128 devices in a mesh: rows: 16 (over x, y), cols: 8 (over z, core).
Axes of the slice: x: 4, y: 4, z: 4, core: 2. Of those that a mesh axis runs over, the one named last changes fastest.
Arguments:
- projection: float32 [8192, 65536], P('rows', 'cols'), may hold values from -0.0625 to 0.0625
- basis: float32 [128, 65536], P(None, ('cols', 'rows')), may hold values from -6 to 6
Outputs:
- new_block: float32 [16, 65536], P(None, ('cols', 'rows'))
- coefficients: float32 [128, 16], replicated
- factor: float32 [16, 16], replicated
The draws below stay inside these ranges and needn't reach their ends.
All inputs are finite; a program needn't handle non-finite values.
Results may differ from the reference program's by a relative error of at most 0.0029.
Values sent between devices are 32-bit elements; how exact they have to be, the bound alone decides.
A program may use at most 64 MiB of HBM per device.

```python
import jax
import jax.numpy as jnp
from jax import lax

N = 65536
BS = 16
BASIS = 128
M = 8192


def levels(own_key, extent, cuts, smallest, top_value):
    factor_of, own = 1.0, jax.random.fold_in(own_key, 6)
    for axis_at, blocks in cuts:
        draws = jnp.exp(jax.random.uniform(jax.random.fold_in(own, axis_at), (blocks,), jnp.float32, smallest / len(cuts), top_value / len(cuts)))
        factor_of = factor_of * jnp.repeat(draws, extent[axis_at] // blocks).reshape([-1 if axis == axis_at else 1 for axis in range(len(extent))])
    return factor_of


def bell_draw(stream_key, shape, deviation, limit, shards=(), dtype=jnp.bfloat16):
    array = jax.random.normal(stream_key, shape, jnp.float32) * deviation
    if len(shards) > 0:
        array = levels(stream_key, shape, shards, -0.22, 0.18) * array
    return jnp.clip(array, min=-limit, max=limit).astype(dtype)


def setup_inputs(seed: int = 0) -> dict:
    arg_keys = jax.random.split(jax.random.key(seed), 3)
    return {
        "projection": bell_draw(arg_keys[0], (M, N), M ** -0.5, 0.0625, ((0, 16), (1, 8)), jnp.float32),
        "basis": bell_draw(arg_keys[1], (BASIS, N), 1.0, 6.0, ((1, 128),), jnp.float32),
    }


def contract(left, right):
    return lax.dot_general(left.astype(jnp.float32), right.astype(jnp.float32), (((1,), (1,)), ((), ())), precision=lax.Precision.HIGHEST, preferred_element_type=jnp.float32)

def reference(projection, basis):
    current = basis[BASIS - BS:]
    projected = contract(current, projection)
    image = jnp.dot(projected, projection, precision=lax.Precision.HIGHEST)
    first_coef = contract(basis, image) / N
    image_one = image - jnp.dot(first_coef.T, basis, precision=lax.Precision.HIGHEST)
    second_coef = contract(basis, image_one) / N
    image_two = image_one - jnp.dot(second_coef.T, basis, precision=lax.Precision.HIGHEST)
    gram_matrix = contract(image_two, image_two) / N
    factor = jnp.linalg.cholesky(gram_matrix)
    new_block = jax.scipy.linalg.solve_triangular(factor, image_two, lower=True)
    return (new_block, first_coef + second_coef, factor)
```

```python
import functools

import jax
import jax.numpy as jnp
from jax import lax
from jax.experimental import pallas as pl
from jax.experimental.pallas import tpu as pltpu
from jax.sharding import PartitionSpec as P

N = 65536
BS = 16
SIDE = 4
LANES = 128
SUB = 8
MESH = pl.DeviceIdType.MESH
f32, bf16 = jnp.float32, jnp.bfloat16
ROW_BY_ROW = (((1,), (1,)), ((), ()))
ROW_BY_COL = (((1,), (0,)), ((), ()))


def product(left, right, dims):
    return lax.dot_general(left, right, dims, preferred_element_type=f32)


def exact(left, right, dims):
    return lax.dot_general(
        left, right, dims, precision=lax.Precision.HIGHEST, preferred_element_type=f32
    )


def two_terms(value):
    high = value.astype(bf16)
    return high, (value - high.astype(f32)).astype(bf16)


def row_after(row, step):
    x, y = row // SIDE, row % SIDE
    return (x + step // SIDE) % SIDE * SIDE + (y + step % SIDE) % SIDE


def row_before(row, step):
    x, y = row // SIDE, row % SIDE
    return (x + SIDE - step // SIDE) % SIDE * SIDE + (y + SIDE - step % SIDE) % SIDE


def arrive(buffer, sem):
    pltpu.make_async_copy(buffer, buffer, sem).wait()


def kernel(
    rows, cols, a_hbm, basis_hbm, new_ref, coef_ref, factor_ref,
    a_all, a_high, a_low, basis, current, acc, tiles, tiles_in, whole,
    image_out, image_in, corr, corr_in, corr_rows, corr_whole, stat_cols, stat_rows,
    a_sem, basis_sem, cur_send, cur_recv, tile_send, tile_recv, whole_send, whole_recv,
    image_send, image_recv, corr_send, corr_recv, crow_send, crow_recv, call_send, call_recv,
    scol_send, scol_recv, srow_send, srow_recv,
):
    row, col = lax.axis_index("rows"), lax.axis_index("cols")
    width = basis.shape[1]
    prior = basis.shape[0]

    def to_row(source, target, send, recv, peer):
        copy = pltpu.make_async_remote_copy(
            source, target, send, recv, device_id={"rows": peer}, device_id_type=MESH
        )
        copy.start()
        return copy

    def to_col(source, target, send, recv, peer):
        copy = pltpu.make_async_remote_copy(
            source, target, send, recv, device_id={"cols": peer}, device_id_type=MESH
        )
        copy.start()
        return copy

    sent = []
    barrier = pltpu.get_barrier_semaphore()
    for step in range(1, rows):
        pl.semaphore_signal(barrier, inc=1, device_id={"rows": row_after(row, step)}, device_id_type=MESH)
    for step in range(1, cols):
        pl.semaphore_signal(barrier, inc=1, device_id={"cols": (col + step) % cols}, device_id_type=MESH)

    last = basis_hbm.at[pl.ds(prior - BS, BS)]
    pltpu.make_async_copy(last, current.at[row], cur_recv.at[row]).start()
    load_basis = pltpu.make_async_copy(basis_hbm, basis, basis_sem)
    load_basis.start()

    @pl.loop(0, rows)
    def _(step):
        source = row_before(row, step)
        columns = pl.ds(pl.multiple_of(source * width, width), width)
        pltpu.make_async_copy(a_hbm.at[:, columns], a_all.at[source], a_sem.at[source]).start()

    pl.semaphore_wait(barrier, rows + cols - 2)

    for step in range(1, rows):
        peer = row_after(row, step)
        sent.append(to_row(last, current.at[row], cur_send.at[step], cur_recv.at[row], peer))

    load_basis.wait()
    share = prior // cols
    corr[...] = (exact(basis[...], basis[...], ROW_BY_ROW) * (1.0 / N)).reshape(cols, share, prior)
    for step in range(1, cols):
        peer = (col + step) % cols
        sent.append(to_col(corr.at[peer], corr_in.at[col], corr_send.at[step], corr_recv.at[col], peer))

    acc[...] = jnp.zeros_like(acc)

    @pl.loop(0, rows)
    def _(step):
        source = row_before(row, step)
        arrive(a_all.at[source], a_sem.at[source])
        arrive(current.at[source], cur_recv.at[source])
        high, low = two_terms(a_all[source])
        a_high[source] = high
        a_low[source] = low
        cur_high, cur_low = two_terms(current[source])
        both = product(jnp.concatenate([cur_high, cur_low], 0), high, ROW_BY_ROW)
        acc[...] += both[:BS] + both[BS:] + product(cur_high, low, ROW_BY_ROW)

    across = acc.shape[1] // LANES
    for t in range(cols):
        tiles[t] = acc[t // across * SUB : (t // across + 1) * SUB, t % across * LANES : (t % across + 1) * LANES]
    for step in range(1, cols):
        peer = (col + step) % cols
        sent.append(to_col(tiles.at[peer], tiles_in.at[col], tile_send.at[step], tile_recv.at[col], peer))

    total = corr[col]
    for step in range(1, cols):
        source = (col + cols - step) % cols
        arrive(corr_in.at[source], corr_recv.at[source])
        total += corr_in[source]
    corr_rows[row] = total
    for step in range(1, rows):
        peer = row_after(row, step)
        sent.append(to_row(corr_rows.at[row], corr_rows.at[row], crow_send.at[step], crow_recv.at[row], peer))

    total = tiles[col]
    for step in range(1, cols):
        source = (col + cols - step) % cols
        arrive(tiles_in.at[source], tile_recv.at[source])
        total += tiles_in[source]
    whole[col] = total
    for step in range(1, cols):
        peer = (col + step) % cols
        sent.append(to_col(whole.at[col], whole.at[col], whole_send.at[step], whole_recv.at[col], peer))
    for step in range(1, cols):
        source = (col + cols - step) % cols
        arrive(whole.at[source], whole_recv.at[source])
    projected = jnp.concatenate(
        [jnp.concatenate([whole[t] for t in range(top * across, (top + 1) * across)], 1) for top in range(BS // SUB)], 0
    )

    pro_high, pro_low = two_terms(projected)
    pro_both = jnp.concatenate([pro_high, pro_low], 0)

    def block(peer):
        both = product(pro_both, a_high[peer], ROW_BY_COL)
        return both[:BS] + both[BS:] + product(pro_high, a_low[peer], ROW_BY_COL)

    @pl.loop(1, rows)
    def _(step):
        peer = row_after(row, step)
        image_out[peer] = block(peer)
        to_row(image_out.at[peer], image_in.at[row], image_send.at[step], image_recv.at[row], peer)

    image = block(row)

    total = jnp.zeros_like(corr_rows[0])
    for source in range(rows):
        @pl.when(source != row)
        def _():
            arrive(corr_rows.at[source], crow_recv.at[source])
        total += corr_rows[source]
    corr_whole[col] = total
    for step in range(1, cols):
        peer = (col + step) % cols
        sent.append(to_col(corr_whole.at[col], corr_whole.at[col], call_send.at[step], call_recv.at[col], peer))

    for step in range(1, rows):
        source = row_before(row, step)
        arrive(image_in.at[source], image_recv.at[source])
        image += image_in[source]

    own = basis[...]
    pairs = exact(image, jnp.concatenate([own, image], 0), ROW_BY_ROW) * (1.0 / N)
    stat_cols[col, :BS] = pairs[:, :prior]
    stat_cols[col, BS:] = jnp.concatenate([pairs[:, prior:], jnp.zeros((BS, prior - BS), f32)], 1)
    for step in range(1, cols):
        peer = (col + step) % cols
        sent.append(to_col(stat_cols.at[col], stat_cols.at[col], scol_send.at[step], scol_recv.at[col], peer))

    for step in range(1, cols):
        source = (col + cols - step) % cols
        arrive(corr_whole.at[source], call_recv.at[source])
    correlation = corr_whole[...].reshape(prior, prior)
    at = lax.broadcasted_iota(jnp.int32, (prior, prior), 0)
    double = jnp.where(at == lax.broadcasted_iota(jnp.int32, (prior, prior), 1), 2.0, 0.0) - correlation
    inner = 2.0 * double - exact(exact(double, correlation, ROW_BY_COL), double, ROW_BY_COL)

    for step in range(1, cols):
        source = (col + cols - step) % cols
        arrive(stat_cols.at[source], scol_recv.at[source])
    total = stat_cols[0]
    for source in range(1, cols):
        total += stat_cols[source]
    stat_rows[row] = total
    for step in range(1, rows):
        peer = row_after(row, step)
        sent.append(to_row(stat_rows.at[row], stat_rows.at[row], srow_send.at[step], srow_recv.at[row], peer))
    for step in range(1, rows):
        source = row_before(row, step)
        arrive(stat_rows.at[source], srow_recv.at[source])
    total = stat_rows[0]
    for source in range(1, rows):
        total += stat_rows[source]

    cross, self_gram = total[:BS], total[BS:, :BS]
    coeffs = exact(cross, double, ROW_BY_ROW)
    gram = self_gram - exact(exact(cross, inner, ROW_BY_ROW), cross, ROW_BY_ROW)
    image -= exact(coeffs, own, ROW_BY_COL)
    coef_ref[...] = coeffs

    line = lax.broadcasted_iota(jnp.int32, (BS, BS), 0)
    lane = lax.broadcasted_iota(jnp.int32, (BS, BS), 1)
    below = lax.broadcasted_iota(jnp.int32, (BS, 1), 0)
    factor = jnp.zeros((BS, BS), f32)
    for j in range(BS):
        column = gram[:, j : j + 1]
        scale = 1.0 / jnp.sqrt(column[j : j + 1])
        column = column * scale
        gram_line = gram[j : j + 1] * scale
        image_line = image[j : j + 1] * scale
        factor = jnp.where((lane == j) & (line >= j), column, factor)
        part = jnp.where(below > j, column, 0.0)
        gram = gram - part * gram_line
        image = jnp.where(below == j, image_line, image - part * image_line)
    new_ref[...] = image
    factor_ref[...] = factor

    for copy in sent:
        copy.wait_send()

    @pl.loop(1, rows)
    def _(step):
        arrive(image_out.at[row_after(row, step)], image_send.at[step])


def local(rows, cols, projection, basis):
    rays, columns = projection.shape
    prior, width = basis.shape
    dma = pltpu.SemaphoreType.DMA
    call = pl.pallas_call(
        functools.partial(kernel, rows, cols),
        out_shape=(
            jax.ShapeDtypeStruct((BS, width), f32),
            jax.ShapeDtypeStruct((BS, prior), f32),
            jax.ShapeDtypeStruct((BS, BS), f32),
        ),
        in_specs=[pl.BlockSpec(memory_space=pltpu.HBM)] * 2,
        out_specs=[pl.BlockSpec(memory_space=pltpu.VMEM)] * 3,
        scratch_shapes=[
            pltpu.VMEM((rows, rays, width), f32),
            pltpu.VMEM((rows, rays, width), bf16),
            pltpu.VMEM((rows, rays, width), bf16),
            pltpu.VMEM((prior, width), f32),
            pltpu.VMEM((rows, BS, width), f32),
            pltpu.VMEM((BS, rays), f32),
            pltpu.VMEM((cols, SUB, LANES), f32),
            pltpu.VMEM((cols, SUB, LANES), f32),
            pltpu.VMEM((cols, SUB, LANES), f32),
            pltpu.VMEM((rows, BS, width), f32),
            pltpu.VMEM((rows, BS, width), f32),
            pltpu.VMEM((cols, prior // cols, prior), f32),
            pltpu.VMEM((cols, prior // cols, prior), f32),
            pltpu.VMEM((rows, prior // cols, prior), f32),
            pltpu.VMEM((cols, prior // cols, prior), f32),
            pltpu.VMEM((cols, 2 * BS, prior), f32),
            pltpu.VMEM((rows, 2 * BS, prior), f32),
            dma((rows,)), dma,
            dma((rows,)), dma((rows,)),
            dma((cols,)), dma((cols,)), dma((cols,)), dma((cols,)),
            dma((rows,)), dma((rows,)),
            dma((cols,)), dma((cols,)), dma((rows,)), dma((rows,)), dma((cols,)), dma((cols,)),
            dma((cols,)), dma((cols,)), dma((rows,)), dma((rows,)),
        ],
        compiler_params=pltpu.CompilerParams(
            collective_id=0, has_side_effects=True, vmem_limit_bytes=48 << 20
        ),
    )
    new_block, coefficients, factor = call(projection, basis)
    return new_block, coefficients.T, factor


def solution(mesh):
    placed = (P("rows", "cols"), P(None, ("cols", "rows")))
    return jax.shard_map(
        functools.partial(local, mesh.shape["rows"], mesh.shape["cols"]),
        mesh=mesh,
        in_specs=placed,
        out_specs=(P(None, ("cols", "rows")), P(), P()),
        check_vma=False,
    )
```

```python
import functools

import jax
import jax.numpy as jnp
from jax import lax
from jax.experimental import pallas as pl
from jax.experimental.pallas import tpu as pltpu
from jax.sharding import PartitionSpec as P

N = 65536
BS = 16
DEPTH = 6
EARLY = 4
SIDE = 4
MESH = pl.DeviceIdType.MESH
BOTH_AXES = [5, 6, 7, 9, 10, 11, 13, 14, 15]
ONE_AXIS = [1, 2, 3, 4, 8, 12]
FAR_FIRST = BOTH_AXES + ONE_AXIS
NEAR_FIRST = ONE_AXIS + BOTH_AXES
f32, bf16 = jnp.float32, jnp.bfloat16
ROW_BY_ROW = (((1,), (1,)), ((), ()))
ROW_BY_COL = (((1,), (0,)), ((), ()))


def product(left, right, dims):
    return lax.dot_general(left, right, dims, preferred_element_type=f32)


def exact(left, right, dims):
    return lax.dot_general(
        left, right, dims, precision=lax.Precision.HIGHEST, preferred_element_type=f32
    )


def two_terms(value):
    high = value.astype(bf16)
    return high, (value - high.astype(f32)).astype(bf16)


def row_after(row, step):
    x, y = row // SIDE, row % SIDE
    return (x + step // SIDE) % SIDE * SIDE + (y + step % SIDE) % SIDE


def row_before(row, step):
    x, y = row // SIDE, row % SIDE
    return (x + SIDE - step // SIDE) % SIDE * SIDE + (y + SIDE - step % SIDE) % SIDE


def near_first(step):
    both = step - 7
    return jnp.where(step < 4, step, jnp.where(step < 7, 4 * (step - 3), 5 + both // 3 * 4 + both % 3))


def far_first(step):
    return near_first((step + 5) % 15 + 1)


def arrive(buffer, sem):
    pltpu.make_async_copy(buffer, buffer, sem).wait()


def kernel(
    rows, cols, a_hbm, basis_hbm, new_ref, coef_ref, factor_ref,
    a_stage, a_high, a_low, a_high_t, a_low_t, basis, current, acc, parts,
    image_out, image_in, corr, corr_in, corr_rows, corr_whole, stat_cols, stat_rows,
    a_sem, basis_sem, cur_send, cur_recv, part_send, part_recv,
    image_send, image_recv, corr_send, corr_recv, crow_send, crow_recv, call_send, call_recv,
    scol_send, scol_recv, srow_send, srow_recv,
):
    row, col = lax.axis_index("rows"), lax.axis_index("cols")
    width = basis.shape[1]
    prior = basis.shape[0]

    def to_row(source, target, send, recv, peer):
        copy = pltpu.make_async_remote_copy(
            source, target, send, recv, device_id={"rows": peer}, device_id_type=MESH
        )
        copy.start()
        return copy

    def to_col(source, target, send, recv, peer):
        copy = pltpu.make_async_remote_copy(
            source, target, send, recv, device_id={"cols": peer}, device_id_type=MESH
        )
        copy.start()
        return copy

    sent = []
    barrier = pltpu.get_barrier_semaphore()
    for step in FAR_FIRST:
        pl.semaphore_signal(barrier, inc=1, device_id={"rows": row_after(row, step)}, device_id_type=MESH)
    for step in range(1, cols):
        pl.semaphore_signal(barrier, inc=1, device_id={"cols": (col + step) % cols}, device_id_type=MESH)

    last = basis_hbm.at[pl.ds(prior - BS, BS)]
    pltpu.make_async_copy(last, current.at[row], cur_recv.at[row]).start()
    load_basis = pltpu.make_async_copy(basis_hbm, basis, basis_sem)
    load_basis.start()

    depth = a_stage.shape[0]

    def fetch(block):
        columns = pl.ds(pl.multiple_of(block * width, width), width)
        slot = block % depth
        return pltpu.make_async_copy(a_hbm.at[:, columns], a_stage.at[slot], a_sem.at[slot])

    def prepare(block):
        fetch(block).wait()
        plain = a_stage[block % depth]
        turned = plain.T
        high, low = two_terms(plain)
        a_high[block] = high
        a_low[block] = low
        high, low = two_terms(turned)
        a_high_t[block] = high
        a_low_t[block] = low

        @pl.when(block + depth < rows)
        def _():
            fetch(block + depth).start()

    for block in range(depth):
        fetch(block).start()

    @pl.loop(0, EARLY)
    def _(block):
        prepare(block)

    arrive(current.at[row], cur_recv.at[row])
    pl.semaphore_wait(barrier, rows + cols - 2)

    for step in FAR_FIRST:
        peer = row_after(row, step)
        sent.append(to_row(current.at[row], current.at[row], cur_send.at[step], cur_recv.at[row], peer))

    load_basis.wait()
    share = prior // cols
    corr[...] = (exact(basis[...], basis[...], ROW_BY_ROW) * (1.0 / N)).reshape(cols, share, prior)
    for step in range(1, cols):
        peer = (col + step) % cols
        sent.append(to_col(corr.at[peer], corr_in.at[col], corr_send.at[step], corr_recv.at[col], peer))

    @pl.loop(EARLY, rows)
    def _(block):
        prepare(block)

    def rays(source):
        cur_high, cur_low = two_terms(current[source])
        both = product(jnp.concatenate([cur_high, cur_low], 0), a_high_t[source], ROW_BY_COL)
        return both[:BS] + both[BS:] + product(cur_high, a_low_t[source], ROW_BY_COL)

    acc[...] = rays(row)

    @pl.loop(1, rows)
    def _(step):
        source = row_before(row, near_first(step))
        arrive(current.at[source], cur_recv.at[source])
        acc[...] += rays(source)

    parts[col] = acc[...]
    for step in range(1, cols):
        peer = (col + step) % cols
        sent.append(to_col(parts.at[col], parts.at[col], part_send.at[step], part_recv.at[col], peer))

    total = corr[col]
    for step in range(1, cols):
        source = (col + cols - step) % cols
        arrive(corr_in.at[source], corr_recv.at[source])
        total += corr_in[source]
    corr_rows[row] = total
    for step in range(1, rows):
        peer = row_after(row, step)
        sent.append(to_row(corr_rows.at[row], corr_rows.at[row], crow_send.at[step], crow_recv.at[row], peer))

    for step in range(1, cols):
        source = (col + cols - step) % cols
        arrive(parts.at[source], part_recv.at[source])
    projected = parts[0]
    for source in range(1, cols):
        projected += parts[source]

    pro_high, pro_low = two_terms(projected)
    pro_both = jnp.concatenate([pro_high, pro_low], 0)

    def block(peer):
        both = product(pro_both, a_high[peer], ROW_BY_COL)
        return both[:BS] + both[BS:] + product(pro_high, a_low[peer], ROW_BY_COL)

    @pl.loop(1, rows)
    def _(step):
        peer = row_after(row, far_first(step))
        image_out[peer] = block(peer)
        to_row(image_out.at[peer], image_in.at[row], image_send.at[step], image_recv.at[row], peer)

    image = block(row)

    total = jnp.zeros_like(corr_rows[0])
    for source in range(rows):
        @pl.when(source != row)
        def _():
            arrive(corr_rows.at[source], crow_recv.at[source])
        total += corr_rows[source]
    corr_whole[col] = total
    for step in range(1, cols):
        peer = (col + step) % cols
        sent.append(to_col(corr_whole.at[col], corr_whole.at[col], call_send.at[step], call_recv.at[col], peer))

    for step in range(1, rows):
        source = row_before(row, step)
        arrive(image_in.at[source], image_recv.at[source])
        image += image_in[source]

    own = basis[...]
    pairs = exact(image, jnp.concatenate([own, image], 0), ROW_BY_ROW) * (1.0 / N)
    stat_cols[col, :BS] = pairs[:, :prior]
    stat_cols[col, BS:] = jnp.concatenate([pairs[:, prior:], jnp.zeros((BS, prior - BS), f32)], 1)
    for step in range(1, cols):
        peer = (col + step) % cols
        sent.append(to_col(stat_cols.at[col], stat_cols.at[col], scol_send.at[step], scol_recv.at[col], peer))

    for step in range(1, cols):
        source = (col + cols - step) % cols
        arrive(corr_whole.at[source], call_recv.at[source])
    correlation = corr_whole[...].reshape(prior, prior)
    at = lax.broadcasted_iota(jnp.int32, (prior, prior), 0)
    double = jnp.where(at == lax.broadcasted_iota(jnp.int32, (prior, prior), 1), 2.0, 0.0) - correlation
    inner = 2.0 * double - exact(exact(double, correlation, ROW_BY_COL), double, ROW_BY_COL)

    for step in range(1, cols):
        source = (col + cols - step) % cols
        arrive(stat_cols.at[source], scol_recv.at[source])
    total = stat_cols[0]
    for source in range(1, cols):
        total += stat_cols[source]
    stat_rows[row] = total
    for step in FAR_FIRST:
        peer = row_after(row, step)
        sent.append(to_row(stat_rows.at[row], stat_rows.at[row], srow_send.at[step], srow_recv.at[row], peer))
    for step in range(1, rows):
        source = row_before(row, step)
        arrive(stat_rows.at[source], srow_recv.at[source])
    total = stat_rows[0]
    for source in range(1, rows):
        total += stat_rows[source]

    cross, self_gram = total[:BS], total[BS:, :BS]
    coeffs = exact(cross, double, ROW_BY_ROW)
    gram = self_gram - exact(exact(cross, inner, ROW_BY_ROW), cross, ROW_BY_ROW)
    image -= exact(coeffs, own, ROW_BY_COL)
    coef_ref[...] = coeffs

    line = lax.broadcasted_iota(jnp.int32, (BS, BS), 0)
    lane = lax.broadcasted_iota(jnp.int32, (BS, BS), 1)
    below = lax.broadcasted_iota(jnp.int32, (BS, 1), 0)
    factor = jnp.zeros((BS, BS), f32)
    for j in range(BS):
        column = gram[:, j : j + 1]
        scale = 1.0 / jnp.sqrt(column[j : j + 1])
        column = column * scale
        gram_line = gram[j : j + 1] * scale
        image_line = image[j : j + 1] * scale
        factor = jnp.where((lane == j) & (line >= j), column, factor)
        part = jnp.where(below > j, column, 0.0)
        gram = gram - part * gram_line
        image = jnp.where(below == j, image_line, image - part * image_line)
    new_ref[...] = image
    factor_ref[...] = factor

    for copy in sent:
        copy.wait_send()

    @pl.loop(1, rows)
    def _(step):
        arrive(image_out.at[row_after(row, step)], image_send.at[step])


def local(rows, cols, projection, basis):
    rays, columns = projection.shape
    prior, width = basis.shape
    dma = pltpu.SemaphoreType.DMA
    call = pl.pallas_call(
        functools.partial(kernel, rows, cols),
        out_shape=(
            jax.ShapeDtypeStruct((BS, width), f32),
            jax.ShapeDtypeStruct((BS, prior), f32),
            jax.ShapeDtypeStruct((BS, BS), f32),
        ),
        in_specs=[pl.BlockSpec(memory_space=pltpu.HBM)] * 2,
        out_specs=[pl.BlockSpec(memory_space=pltpu.VMEM)] * 3,
        scratch_shapes=[
            pltpu.VMEM((DEPTH, rays, width), f32),
            pltpu.VMEM((rows, rays, width), bf16),
            pltpu.VMEM((rows, rays, width), bf16),
            pltpu.VMEM((rows, width, rays), bf16),
            pltpu.VMEM((rows, width, rays), bf16),
            pltpu.VMEM((prior, width), f32),
            pltpu.VMEM((rows, BS, width), f32),
            pltpu.VMEM((BS, rays), f32),
            pltpu.VMEM((cols, BS, rays), f32),
            pltpu.VMEM((rows, BS, width), f32),
            pltpu.VMEM((rows, BS, width), f32),
            pltpu.VMEM((cols, prior // cols, prior), f32),
            pltpu.VMEM((cols, prior // cols, prior), f32),
            pltpu.VMEM((rows, prior // cols, prior), f32),
            pltpu.VMEM((cols, prior // cols, prior), f32),
            pltpu.VMEM((cols, 2 * BS, prior), f32),
            pltpu.VMEM((rows, 2 * BS, prior), f32),
            dma((DEPTH,)), dma,
            dma((rows,)), dma((rows,)),
            dma((cols,)), dma((cols,)),
            dma((rows,)), dma((rows,)),
            dma((cols,)), dma((cols,)), dma((rows,)), dma((rows,)), dma((cols,)), dma((cols,)),
            dma((cols,)), dma((cols,)), dma((rows,)), dma((rows,)),
        ],
        compiler_params=pltpu.CompilerParams(
            collective_id=0, has_side_effects=True, vmem_limit_bytes=48 << 20
        ),
    )
    new_block, coefficients, factor = call(projection, basis)
    return new_block, coefficients.T, factor


def solution(mesh):
    placed = (P("rows", "cols"), P(None, ("cols", "rows")))
    return jax.shard_map(
        functools.partial(local, mesh.shape["rows"], mesh.shape["cols"]),
        mesh=mesh,
        in_specs=placed,
        out_specs=(P(None, ("cols", "rows")), P(), P()),
        check_vma=False,
    )
```

```python
import functools

import jax
import jax.numpy as jnp
from jax import lax
from jax.experimental import pallas as pl
from jax.experimental.pallas import tpu as pltpu
from jax.sharding import PartitionSpec as P

N = 65536
BS = 16
DEPTH = 6
EARLY = 4
LAST = 6
SIDE = 4
MESH = pl.DeviceIdType.MESH
FAR_FIRST = [10, 6, 9, 14, 11, 5, 7, 13, 15, 8, 2, 1, 3, 4, 12]
f32, bf16 = jnp.float32, jnp.bfloat16
ROW_BY_ROW = (((1,), (1,)), ((), ()))
ROW_BY_COL = (((1,), (0,)), ((), ()))


def product(left, right, dims):
    return lax.dot_general(left, right, dims, preferred_element_type=f32)


def exact(left, right, dims):
    return lax.dot_general(
        left, right, dims, precision=lax.Precision.HIGHEST, preferred_element_type=f32
    )


def two_terms(value):
    high = value.astype(bf16)
    return high, (value - high.astype(f32)).astype(bf16)


def row_after(row, step):
    x, y = row // SIDE, row % SIDE
    return (x + step // SIDE) % SIDE * SIDE + (y + step % SIDE) % SIDE


def row_before(row, step):
    x, y = row // SIDE, row % SIDE
    return (x + SIDE - step // SIDE) % SIDE * SIDE + (y + SIDE - step % SIDE) % SIDE


def far_first(step):
    place = 0
    for k, at in enumerate(FAR_FIRST):
        place = jnp.where(step == k + 1, at, place)
    return place


def arrive(buffer, sem):
    pltpu.make_async_copy(buffer, buffer, sem).wait()


def kernel(
    rows, cols, a_hbm, basis_hbm, new_ref, coef_ref, factor_ref,
    a_stage, a_high, a_low, a_high_t, a_low_t, basis, current, acc, parts,
    image_out, image_in, corr, corr_in, corr_rows, corr_whole, stat_cols, stat_rows, squares,
    a_sem, basis_sem, cur_send, cur_recv, part_send, part_recv,
    image_send, image_recv, corr_send, corr_recv, crow_send, crow_recv, call_send, call_recv,
    scol_send, scol_recv, srow_send, srow_recv, square_send, square_recv,
):
    row, col = lax.axis_index("rows"), lax.axis_index("cols")
    width = basis.shape[1]
    prior = basis.shape[0]

    def to_row(source, target, send, recv, peer):
        copy = pltpu.make_async_remote_copy(
            source, target, send, recv, device_id={"rows": peer}, device_id_type=MESH
        )
        copy.start()
        return copy

    def to_col(source, target, send, recv, peer):
        copy = pltpu.make_async_remote_copy(
            source, target, send, recv, device_id={"cols": peer}, device_id_type=MESH
        )
        copy.start()
        return copy

    sent = []
    barrier = pltpu.get_barrier_semaphore()
    for step in FAR_FIRST:
        pl.semaphore_signal(barrier, inc=1, device_id={"rows": row_after(row, step)}, device_id_type=MESH)
    for step in range(1, cols):
        pl.semaphore_signal(barrier, inc=1, device_id={"cols": (col + step) % cols}, device_id_type=MESH)

    last = basis_hbm.at[pl.ds(prior - BS, BS)]
    pltpu.make_async_copy(last, current.at[row], cur_recv.at[row]).start()
    load_basis = pltpu.make_async_copy(basis_hbm, basis, basis_sem)
    load_basis.start()

    depth = a_stage.shape[0]

    def fetch(block):
        columns = pl.ds(pl.multiple_of(block * width, width), width)
        slot = block % depth
        return pltpu.make_async_copy(a_hbm.at[:, columns], a_stage.at[slot], a_sem.at[slot])

    def prepare(block):
        fetch(block).wait()
        plain = a_stage[block % depth]
        turned = plain.T
        high, low = two_terms(plain)
        a_high[block] = high
        a_low[block] = low
        high, low = two_terms(turned)
        a_high_t[block] = high
        a_low_t[block] = low

        @pl.when(block + depth < rows)
        def _():
            fetch(block + depth).start()

    for block in range(depth):
        fetch(block).start()

    @pl.loop(0, EARLY)
    def _(block):
        prepare(block)

    arrive(current.at[row], cur_recv.at[row])
    pl.semaphore_wait(barrier, rows + cols - 2)

    for step in FAR_FIRST:
        peer = row_after(row, step)
        sent.append(to_row(current.at[row], current.at[row], cur_send.at[step], cur_recv.at[row], peer))

    load_basis.wait()
    share = prior // cols
    corr[...] = (exact(basis[...], basis[...], ROW_BY_ROW) * (1.0 / N)).reshape(cols, share, prior)
    for step in range(1, cols):
        peer = (col + step) % cols
        sent.append(to_col(corr.at[peer], corr_in.at[col], corr_send.at[step], corr_recv.at[col], peer))

    @pl.loop(EARLY, rows)
    def _(block):
        prepare(block)

    half = acc.shape[1] // 2

    def rays(source, columns):
        cur_high, cur_low = two_terms(current[source])
        both = product(jnp.concatenate([cur_high, cur_low], 0), a_high_t[source, :, columns], ROW_BY_COL)
        return both[:BS] + both[BS:] + product(cur_high, a_low_t[source, :, columns], ROW_BY_COL)

    acc[...] = rays(row, slice(None))

    @pl.loop(1, rows - LAST)
    def _(step):
        source = row_before(row, far_first(step))
        arrive(current.at[source], cur_recv.at[source])
        acc[...] += rays(source, slice(None))

    for part in range(2):
        columns = slice(part * half, (part + 1) * half)
        total = acc[:, columns]
        for step in FAR_FIRST[rows - LAST - 1 :]:
            source = row_before(row, step)
            if part == 0:
                arrive(current.at[source], cur_recv.at[source])
            total += rays(source, columns)
        parts[part, col] = total
        for step in range(1, cols):
            peer = (col + step) % cols
            sent.append(to_col(parts.at[part, col], parts.at[part, col], part_send.at[part, step], part_recv.at[part, col], peer))

    total = corr[col]
    for step in range(1, cols):
        source = (col + cols - step) % cols
        arrive(corr_in.at[source], corr_recv.at[source])
        total += corr_in[source]
    corr_rows[row] = total
    for step in range(1, rows):
        peer = row_after(row, step)
        sent.append(to_row(corr_rows.at[row], corr_rows.at[row], crow_send.at[step], crow_recv.at[row], peer))

    halves = []
    for part in range(2):
        for step in range(1, cols):
            source = (col + cols - step) % cols
            arrive(parts.at[part, source], part_recv.at[part, source])
        total = parts[part, 0]
        for source in range(1, cols):
            total += parts[part, source]
        halves.append(total)
    projected = jnp.concatenate(halves, 1)

    pro_high, pro_low = two_terms(projected)
    pro_both = jnp.concatenate([pro_high, pro_low], 0)

    def block(peer):
        both = product(pro_both, a_high[peer], ROW_BY_COL)
        return both[:BS] + both[BS:] + product(pro_high, a_low[peer], ROW_BY_COL)

    @pl.loop(1, rows)
    def _(step):
        peer = row_after(row, far_first(step))
        image_out[peer] = block(peer)
        to_row(image_out.at[peer], image_in.at[row], image_send.at[step], image_recv.at[row], peer)

    image = block(row)

    total = jnp.zeros_like(corr_rows[0])
    for source in range(rows):
        @pl.when(source != row)
        def _():
            arrive(corr_rows.at[source], crow_recv.at[source])
        total += corr_rows[source]
    corr_whole[col] = total
    for step in range(1, cols):
        peer = (col + step) % cols
        sent.append(to_col(corr_whole.at[col], corr_whole.at[col], call_send.at[step], call_recv.at[col], peer))

    for step in range(1, rows):
        source = row_before(row, step)
        arrive(image_in.at[source], image_recv.at[source])
        image += image_in[source]

    own = basis[...]
    stat_cols[col] = exact(image, jnp.concatenate([own[: prior - BS], image], 0), ROW_BY_ROW) * (1.0 / N)
    for step in range(1, cols):
        peer = (col + step) % cols
        sent.append(to_col(stat_cols.at[col], stat_cols.at[col], scol_send.at[step], scol_recv.at[col], peer))

    square = exact(projected, projected, ROW_BY_ROW) * (1.0 / N)
    squares[row] = jnp.concatenate([square, jnp.zeros((BS, prior - BS), f32)], 1)
    for step in FAR_FIRST:
        peer = row_after(row, step)
        sent.append(to_row(squares.at[row], squares.at[row], square_send.at[step], square_recv.at[row], peer))

    for step in range(1, cols):
        source = (col + cols - step) % cols
        arrive(corr_whole.at[source], call_recv.at[source])
    correlation = corr_whole[...].reshape(prior, prior)
    at = lax.broadcasted_iota(jnp.int32, (prior, prior), 0)
    double = jnp.where(at == lax.broadcasted_iota(jnp.int32, (prior, prior), 1), 2.0, 0.0) - correlation
    inner = 2.0 * double - exact(exact(double, correlation, ROW_BY_COL), double, ROW_BY_COL)

    for step in range(1, cols):
        source = (col + cols - step) % cols
        arrive(stat_cols.at[source], scol_recv.at[source])
    total = stat_cols[0]
    for source in range(1, cols):
        total += stat_cols[source]
    stat_rows[row] = total
    for step in FAR_FIRST:
        peer = row_after(row, step)
        sent.append(to_row(stat_rows.at[row], stat_rows.at[row], srow_send.at[step], srow_recv.at[row], peer))
    for step in range(1, rows):
        source = row_before(row, step)
        arrive(stat_rows.at[source], srow_recv.at[source])
        arrive(squares.at[source], square_recv.at[source])
    total = stat_rows[0]
    for source in range(1, rows):
        total += stat_rows[source]

    square = squares[0]
    for source in range(1, rows):
        square += squares[source]
    cross = jnp.concatenate([total[:, : prior - BS], square[:, :BS]], 1)
    self_gram = total[:, prior - BS :]
    coeffs = exact(cross, double, ROW_BY_ROW)
    gram = self_gram - exact(exact(cross, inner, ROW_BY_ROW), cross, ROW_BY_ROW)
    image -= exact(coeffs, own, ROW_BY_COL)
    coef_ref[...] = coeffs

    line = lax.broadcasted_iota(jnp.int32, (BS, BS), 0)
    lane = lax.broadcasted_iota(jnp.int32, (BS, BS), 1)
    below = lax.broadcasted_iota(jnp.int32, (BS, 1), 0)
    factor = jnp.zeros((BS, BS), f32)
    for j in range(BS):
        column = gram[:, j : j + 1]
        scale = 1.0 / jnp.sqrt(column[j : j + 1])
        column = column * scale
        gram_line = gram[j : j + 1] * scale
        image_line = image[j : j + 1] * scale
        factor = jnp.where((lane == j) & (line >= j), column, factor)
        part = jnp.where(below > j, column, 0.0)
        gram = gram - part * gram_line
        image = jnp.where(below == j, image_line, image - part * image_line)
    new_ref[...] = image
    factor_ref[...] = factor

    for copy in sent:
        copy.wait_send()

    @pl.loop(1, rows)
    def _(step):
        arrive(image_out.at[row_after(row, step)], image_send.at[step])


def local(rows, cols, projection, basis):
    rays, columns = projection.shape
    prior, width = basis.shape
    dma = pltpu.SemaphoreType.DMA
    call = pl.pallas_call(
        functools.partial(kernel, rows, cols),
        out_shape=(
            jax.ShapeDtypeStruct((BS, width), f32),
            jax.ShapeDtypeStruct((BS, prior), f32),
            jax.ShapeDtypeStruct((BS, BS), f32),
        ),
        in_specs=[pl.BlockSpec(memory_space=pltpu.HBM)] * 2,
        out_specs=[pl.BlockSpec(memory_space=pltpu.VMEM)] * 3,
        scratch_shapes=[
            pltpu.VMEM((DEPTH, rays, width), f32),
            pltpu.VMEM((rows, rays, width), bf16),
            pltpu.VMEM((rows, rays, width), bf16),
            pltpu.VMEM((rows, width, rays), bf16),
            pltpu.VMEM((rows, width, rays), bf16),
            pltpu.VMEM((prior, width), f32),
            pltpu.VMEM((rows, BS, width), f32),
            pltpu.VMEM((BS, rays), f32),
            pltpu.VMEM((2, cols, BS, rays // 2), f32),
            pltpu.VMEM((rows, BS, width), f32),
            pltpu.VMEM((rows, BS, width), f32),
            pltpu.VMEM((cols, prior // cols, prior), f32),
            pltpu.VMEM((cols, prior // cols, prior), f32),
            pltpu.VMEM((rows, prior // cols, prior), f32),
            pltpu.VMEM((cols, prior // cols, prior), f32),
            pltpu.VMEM((cols, BS, prior), f32),
            pltpu.VMEM((rows, BS, prior), f32),
            pltpu.VMEM((rows, BS, prior), f32),
            dma((DEPTH,)), dma,
            dma((rows,)), dma((rows,)),
            dma((2, cols)), dma((2, cols)),
            dma((rows,)), dma((rows,)),
            dma((cols,)), dma((cols,)), dma((rows,)), dma((rows,)), dma((cols,)), dma((cols,)),
            dma((cols,)), dma((cols,)), dma((rows,)), dma((rows,)), dma((rows,)), dma((rows,)),
        ],
        compiler_params=pltpu.CompilerParams(
            collective_id=0, has_side_effects=True, vmem_limit_bytes=55040 << 10
        ),
    )
    new_block, coefficients, factor = call(projection, basis)
    return new_block, coefficients.T, factor


def solution(mesh):
    placed = (P("rows", "cols"), P(None, ("cols", "rows")))
    return jax.shard_map(
        functools.partial(local, mesh.shape["rows"], mesh.shape["cols"]),
        mesh=mesh,
        in_specs=placed,
        out_specs=(P(None, ("cols", "rows")), P(), P()),
        check_vma=False,
    )
```

```python
import functools

import jax
import jax.numpy as jnp
from jax import lax
from jax.experimental import pallas as pl
from jax.experimental.pallas import tpu as pltpu
from jax.sharding import PartitionSpec as P

N = 65536
BS = 16
DEPTH = 6
EARLY = 3
LAST = 6
GROUP = 3
GROUP_OUT = 2
SIDE = 4
MESH = pl.DeviceIdType.MESH
FAR_FIRST = [10, 6, 9, 14, 11, 5, 7, 13, 15, 8, 2, 1, 3, 4, 12]
f32, bf16 = jnp.float32, jnp.bfloat16
ROW_BY_ROW = (((1,), (1,)), ((), ()))
ROW_BY_COL = (((1,), (0,)), ((), ()))


def product(left, right, dims):
    return lax.dot_general(left, right, dims, preferred_element_type=f32)


def exact(left, right, dims):
    return lax.dot_general(
        left, right, dims, precision=lax.Precision.HIGHEST, preferred_element_type=f32
    )


def two_terms(value):
    high = value.astype(bf16)
    return high, (value - high.astype(f32)).astype(bf16)


def row_after(row, step):
    x, y = row // SIDE, row % SIDE
    return (x + step // SIDE) % SIDE * SIDE + (y + step % SIDE) % SIDE


def row_before(row, step):
    x, y = row // SIDE, row % SIDE
    return (x + SIDE - step // SIDE) % SIDE * SIDE + (y + SIDE - step % SIDE) % SIDE


def far_first(step):
    place = 0
    for k, at in enumerate(FAR_FIRST):
        place = jnp.where(step == k + 1, at, place)
    return place


def arrive(buffer, sem):
    pltpu.make_async_copy(buffer, buffer, sem).wait()


def kernel(
    rows, cols, a_hbm, basis_hbm, new_ref, coef_ref, factor_ref,
    a_stage, a_high, a_low, a_high_t, a_low_t, basis, current, acc, parts,
    image_out, image_in, corr, corr_in, corr_rows, corr_whole, stat_cols, stat_rows, squares,
    a_sem, basis_sem, cur_send, cur_recv, part_send, part_recv,
    image_send, image_recv, corr_send, corr_recv, crow_send, crow_recv, call_send, call_recv,
    scol_send, scol_recv, srow_send, srow_recv, square_send, square_recv,
):
    row, col = lax.axis_index("rows"), lax.axis_index("cols")
    width = basis.shape[1]
    prior = basis.shape[0]

    def to_row(source, target, send, recv, peer):
        copy = pltpu.make_async_remote_copy(
            source, target, send, recv, device_id={"rows": peer}, device_id_type=MESH
        )
        copy.start()
        return copy

    def to_col(source, target, send, recv, peer):
        copy = pltpu.make_async_remote_copy(
            source, target, send, recv, device_id={"cols": peer}, device_id_type=MESH
        )
        copy.start()
        return copy

    sent = []
    barrier = pltpu.get_barrier_semaphore()
    for step in FAR_FIRST:
        pl.semaphore_signal(barrier, inc=1, device_id={"rows": row_after(row, step)}, device_id_type=MESH)
    for step in range(1, cols):
        pl.semaphore_signal(barrier, inc=1, device_id={"cols": (col + step) % cols}, device_id_type=MESH)

    last = basis_hbm.at[pl.ds(prior - BS, BS)]
    pltpu.make_async_copy(last, current.at[row], cur_recv.at[row]).start()
    load_basis = pltpu.make_async_copy(basis_hbm, basis, basis_sem)
    load_basis.start()

    depth = a_stage.shape[0]

    def fetch(block):
        columns = pl.ds(pl.multiple_of(block * width, width), width)
        slot = block % depth
        return pltpu.make_async_copy(a_hbm.at[:, columns], a_stage.at[slot], a_sem.at[slot])

    def prepare(block):
        fetch(block).wait()
        plain = a_stage[block % depth]
        turned = plain.T
        high, low = two_terms(plain)
        a_high[block] = high
        a_low[block] = low
        high, low = two_terms(turned)
        a_high_t[block] = high
        a_low_t[block] = low

        @pl.when(block + depth < rows)
        def _():
            fetch(block + depth).start()

    for block in range(depth):
        fetch(block).start()

    @pl.loop(0, EARLY)
    def _(block):
        prepare(block)

    arrive(current.at[row], cur_recv.at[row])
    pl.semaphore_wait(barrier, rows + cols - 2)

    for step in FAR_FIRST:
        peer = row_after(row, step)
        sent.append(to_row(current.at[row], current.at[row], cur_send.at[step], cur_recv.at[row], peer))

    load_basis.wait()
    share = prior // cols
    corr[...] = (exact(basis[...], basis[...], ROW_BY_ROW) * (1.0 / N)).reshape(cols, share, prior)
    for step in range(1, cols):
        peer = (col + step) % cols
        sent.append(to_col(corr.at[peer], corr_in.at[col], corr_send.at[step], corr_recv.at[col], peer))

    @pl.loop(EARLY, rows)
    def _(block):
        prepare(block)

    half = acc.shape[1] // 2

    def rays(source, columns):
        cur_high, cur_low = two_terms(current[source])
        both = product(jnp.concatenate([cur_high, cur_low], 0), a_high_t[source, :, columns], ROW_BY_COL)
        return both[:BS] + both[BS:] + product(cur_high, a_low_t[source, :, columns], ROW_BY_COL)

    acc[...] = rays(row, slice(None))

    @pl.loop(0, (rows - 1 - LAST) // GROUP)
    def _(group):
        sources = [row_before(row, far_first(group * GROUP + k + 1)) for k in range(GROUP)]
        for source in sources:
            arrive(current.at[source], cur_recv.at[source])
        total = acc[...]
        for source in sources:
            total += rays(source, slice(None))
        acc[...] = total

    sources = [row_before(row, step) for step in FAR_FIRST[rows - LAST - 1 :]]
    for source in sources:
        arrive(current.at[source], cur_recv.at[source])

    @pl.loop(0, 2)
    def _(part):
        columns = pl.ds(pl.multiple_of(part * half, half), half)
        total = acc[:, columns]
        for source in sources:
            total += rays(source, columns)
        parts[part, col] = total

        @pl.loop(1, cols)
        def _(step):
            to_col(parts.at[part, col], parts.at[part, col], part_send.at[part, step], part_recv.at[part, col], (col + step) % cols)

    total = corr[col]
    for step in range(1, cols):
        source = (col + cols - step) % cols
        arrive(corr_in.at[source], corr_recv.at[source])
        total += corr_in[source]
    corr_rows[row] = total
    for step in range(1, rows):
        peer = row_after(row, step)
        sent.append(to_row(corr_rows.at[row], corr_rows.at[row], crow_send.at[step], crow_recv.at[row], peer))

    halves = []
    for part in range(2):
        for step in range(1, cols):
            source = (col + cols - step) % cols
            arrive(parts.at[part, source], part_recv.at[part, source])
        total = parts[part, 0]
        for source in range(1, cols):
            total += parts[part, source]
        halves.append(total)
    projected = jnp.concatenate(halves, 1)

    pro_high, pro_low = two_terms(projected)
    pro_both = jnp.concatenate([pro_high, pro_low], 0)

    def block(peer):
        both = product(pro_both, a_high[peer], ROW_BY_COL)
        return both[:BS] + both[BS:] + product(pro_high, a_low[peer], ROW_BY_COL)

    @pl.loop(0, rows // GROUP_OUT)
    def _(group):
        steps = [group * GROUP_OUT + k + 1 for k in range(GROUP_OUT)]
        peers = [row_after(row, far_first(step)) for step in steps]
        for peer in peers:
            image_out[peer] = block(peer)
        for step, peer in zip(steps, peers):
            @pl.when(peer != row)
            def _():
                to_row(image_out.at[peer], image_in.at[row], image_send.at[step], image_recv.at[row], peer)

    total = jnp.zeros_like(corr_rows[0])
    for source in range(rows):
        @pl.when(source != row)
        def _():
            arrive(corr_rows.at[source], crow_recv.at[source])
        total += corr_rows[source]
    corr_whole[col] = total
    for step in range(1, cols):
        peer = (col + step) % cols
        sent.append(to_col(corr_whole.at[col], corr_whole.at[col], call_send.at[step], call_recv.at[col], peer))

    image = image_out[row]
    for step in range(1, rows):
        source = row_before(row, step)
        arrive(image_in.at[source], image_recv.at[source])
        image += image_in[source]

    own = basis[...]
    stat_cols[col] = exact(image, jnp.concatenate([own[: prior - BS], image], 0), ROW_BY_ROW) * (1.0 / N)
    for step in range(1, cols):
        peer = (col + step) % cols
        sent.append(to_col(stat_cols.at[col], stat_cols.at[col], scol_send.at[step], scol_recv.at[col], peer))

    square = exact(projected, projected, ROW_BY_ROW) * (1.0 / N)
    squares[row] = jnp.concatenate([square, jnp.zeros((BS, prior - BS), f32)], 1)
    for step in FAR_FIRST:
        peer = row_after(row, step)
        sent.append(to_row(squares.at[row], squares.at[row], square_send.at[step], square_recv.at[row], peer))

    for step in range(1, cols):
        source = (col + cols - step) % cols
        arrive(corr_whole.at[source], call_recv.at[source])
    correlation = corr_whole[...].reshape(prior, prior)
    at = lax.broadcasted_iota(jnp.int32, (prior, prior), 0)
    double = jnp.where(at == lax.broadcasted_iota(jnp.int32, (prior, prior), 1), 2.0, 0.0) - correlation
    inner = 2.0 * double - exact(exact(double, correlation, ROW_BY_COL), double, ROW_BY_COL)

    for step in range(1, cols):
        source = (col + cols - step) % cols
        arrive(stat_cols.at[source], scol_recv.at[source])
    total = stat_cols[0]
    for source in range(1, cols):
        total += stat_cols[source]
    stat_rows[row] = total
    for step in FAR_FIRST:
        peer = row_after(row, step)
        sent.append(to_row(stat_rows.at[row], stat_rows.at[row], srow_send.at[step], srow_recv.at[row], peer))
    for step in range(1, rows):
        source = row_before(row, step)
        arrive(stat_rows.at[source], srow_recv.at[source])
        arrive(squares.at[source], square_recv.at[source])
    total = stat_rows[0]
    for source in range(1, rows):
        total += stat_rows[source]

    square = squares[0]
    for source in range(1, rows):
        square += squares[source]
    cross = jnp.concatenate([total[:, : prior - BS], square[:, :BS]], 1)
    self_gram = total[:, prior - BS :]
    coeffs = exact(cross, double, ROW_BY_ROW)
    gram = self_gram - exact(exact(cross, inner, ROW_BY_ROW), cross, ROW_BY_ROW)
    image -= exact(coeffs, own, ROW_BY_COL)
    coef_ref[...] = coeffs

    line = lax.broadcasted_iota(jnp.int32, (BS, BS), 0)
    lane = lax.broadcasted_iota(jnp.int32, (BS, BS), 1)
    below = lax.broadcasted_iota(jnp.int32, (BS, 1), 0)
    factor = jnp.zeros((BS, BS), f32)
    for j in range(BS):
        column = gram[:, j : j + 1]
        scale = 1.0 / jnp.sqrt(column[j : j + 1])
        column = column * scale
        gram_line = gram[j : j + 1] * scale
        image_line = image[j : j + 1] * scale
        factor = jnp.where((lane == j) & (line >= j), column, factor)
        part = jnp.where(below > j, column, 0.0)
        gram = gram - part * gram_line
        image = jnp.where(below == j, image_line, image - part * image_line)
    new_ref[...] = image
    factor_ref[...] = factor

    for copy in sent:
        copy.wait_send()

    @pl.loop(1, cols)
    def _(step):
        for part in range(2):
            arrive(parts.at[part, col], part_send.at[part, step])

    @pl.loop(1, rows)
    def _(step):
        arrive(image_out.at[row_after(row, step)], image_send.at[step])


def local(rows, cols, projection, basis):
    rays, columns = projection.shape
    prior, width = basis.shape
    dma = pltpu.SemaphoreType.DMA
    call = pl.pallas_call(
        functools.partial(kernel, rows, cols),
        out_shape=(
            jax.ShapeDtypeStruct((BS, width), f32),
            jax.ShapeDtypeStruct((BS, prior), f32),
            jax.ShapeDtypeStruct((BS, BS), f32),
        ),
        in_specs=[pl.BlockSpec(memory_space=pltpu.HBM)] * 2,
        out_specs=[pl.BlockSpec(memory_space=pltpu.VMEM)] * 3,
        scratch_shapes=[
            pltpu.VMEM((DEPTH, rays, width), f32),
            pltpu.VMEM((rows, rays, width), bf16),
            pltpu.VMEM((rows, rays, width), bf16),
            pltpu.VMEM((rows, width, rays), bf16),
            pltpu.VMEM((rows, width, rays), bf16),
            pltpu.VMEM((prior, width), f32),
            pltpu.VMEM((rows, BS, width), f32),
            pltpu.VMEM((BS, rays), f32),
            pltpu.VMEM((2, cols, BS, rays // 2), f32),
            pltpu.VMEM((rows, BS, width), f32),
            pltpu.VMEM((rows, BS, width), f32),
            pltpu.VMEM((cols, prior // cols, prior), f32),
            pltpu.VMEM((cols, prior // cols, prior), f32),
            pltpu.VMEM((rows, prior // cols, prior), f32),
            pltpu.VMEM((cols, prior // cols, prior), f32),
            pltpu.VMEM((cols, BS, prior), f32),
            pltpu.VMEM((rows, BS, prior), f32),
            pltpu.VMEM((rows, BS, prior), f32),
            dma((DEPTH,)), dma,
            dma((rows,)), dma((rows,)),
            dma((2, cols)), dma((2, cols)),
            dma((rows,)), dma((rows,)),
            dma((cols,)), dma((cols,)), dma((rows,)), dma((rows,)), dma((cols,)), dma((cols,)),
            dma((cols,)), dma((cols,)), dma((rows,)), dma((rows,)), dma((rows,)), dma((rows,)),
        ],
        compiler_params=pltpu.CompilerParams(
            collective_id=0, has_side_effects=True, vmem_limit_bytes=55040 << 10
        ),
    )
    new_block, coefficients, factor = call(projection, basis)
    return new_block, coefficients.T, factor


def solution(mesh):
    placed = (P("rows", "cols"), P(None, ("cols", "rows")))
    return jax.shard_map(
        functools.partial(local, mesh.shape["rows"], mesh.shape["cols"]),
        mesh=mesh,
        in_specs=placed,
        out_specs=(P(None, ("cols", "rows")), P(), P()),
        check_vma=False,
    )
```

```python
import functools

import jax
import jax.numpy as jnp
from jax import lax
from jax.experimental import pallas as pl
from jax.experimental.pallas import tpu as pltpu
from jax.sharding import PartitionSpec as P

N = 65536
BS = 16
DEPTH = 6
EARLY = 3
LAST = 6
GROUP = 3
GROUP_OUT = 2
SIDE = 4
MESH = pl.DeviceIdType.MESH
FAR_FIRST = [10, 6, 9, 14, 11, 5, 7, 13, 15, 8, 2, 1, 3, 4, 12]
f32, bf16 = jnp.float32, jnp.bfloat16
ROW_BY_ROW = (((1,), (1,)), ((), ()))
ROW_BY_COL = (((1,), (0,)), ((), ()))


def product(left, right, dims):
    return lax.dot_general(left, right, dims, preferred_element_type=f32)


def exact(left, right, dims):
    return lax.dot_general(
        left, right, dims, precision=lax.Precision.HIGHEST, preferred_element_type=f32
    )


def two_terms(value):
    high = value.astype(bf16)
    return high, (value - high.astype(f32)).astype(bf16)


def row_after(row, step):
    x, y = row // SIDE, row % SIDE
    return (x + step // SIDE) % SIDE * SIDE + (y + step % SIDE) % SIDE


def row_before(row, step):
    x, y = row // SIDE, row % SIDE
    return (x + SIDE - step // SIDE) % SIDE * SIDE + (y + SIDE - step % SIDE) % SIDE


def far_first(step):
    place = 0
    for k, at in enumerate(FAR_FIRST):
        place = jnp.where(step == k + 1, at, place)
    return place


def arrive(buffer, sem):
    pltpu.make_async_copy(buffer, buffer, sem).wait()


def kernel(
    rows, cols, a_hbm, basis_hbm, new_ref, coef_ref, factor_ref,
    a_stage, a_high, a_low, a_high_t, a_low_t, basis, current, acc, parts,
    image_out, image_in, corr, corr_in, corr_rows, corr_whole, stat_cols, stat_rows, squares,
    a_sem, basis_sem, cur_send, cur_recv, part_send, part_recv,
    image_send, image_recv, corr_send, corr_recv, crow_send, crow_recv, call_send, call_recv,
    scol_send, scol_recv, srow_send, srow_recv, square_send, square_recv,
):
    row, col = lax.axis_index("rows"), lax.axis_index("cols")
    width = basis.shape[1]
    prior = basis.shape[0]

    def to_row(source, target, send, recv, peer):
        copy = pltpu.make_async_remote_copy(
            source, target, send, recv, device_id={"rows": peer}, device_id_type=MESH
        )
        copy.start()
        return copy

    def to_col(source, target, send, recv, peer):
        copy = pltpu.make_async_remote_copy(
            source, target, send, recv, device_id={"cols": peer}, device_id_type=MESH
        )
        copy.start()
        return copy

    sent = []
    barrier = pltpu.get_barrier_semaphore()
    for step in FAR_FIRST:
        pl.semaphore_signal(barrier, inc=1, device_id={"rows": row_after(row, step)}, device_id_type=MESH)
    for step in range(1, cols):
        pl.semaphore_signal(barrier, inc=1, device_id={"cols": (col + step) % cols}, device_id_type=MESH)

    last = basis_hbm.at[pl.ds(prior - BS, BS)]
    pltpu.make_async_copy(last, current.at[row], cur_recv.at[row]).start()
    load_basis = pltpu.make_async_copy(basis_hbm, basis, basis_sem)
    load_basis.start()

    depth = a_stage.shape[0]

    def fetch(block):
        columns = pl.ds(pl.multiple_of(block * width, width), width)
        slot = block % depth
        return pltpu.make_async_copy(a_hbm.at[:, columns], a_stage.at[slot], a_sem.at[slot])

    def prepare(block):
        fetch(block).wait()
        plain = a_stage[block % depth]
        turned = plain.T
        high, low = two_terms(plain)
        a_high[block] = high
        a_low[block] = low
        high, low = two_terms(turned)
        a_high_t[block] = high
        a_low_t[block] = low

        @pl.when(block + depth < rows)
        def _():
            fetch(block + depth).start()

    for block in range(depth):
        fetch(block).start()

    @pl.loop(0, EARLY)
    def _(block):
        prepare(block)

    arrive(current.at[row], cur_recv.at[row])
    pl.semaphore_wait(barrier, rows + cols - 2)

    for step in FAR_FIRST:
        peer = row_after(row, step)
        sent.append(to_row(current.at[row], current.at[row], cur_send.at[step], cur_recv.at[row], peer))

    load_basis.wait()
    share = prior // cols
    corr[...] = (exact(basis[...], basis[...], ROW_BY_ROW) * (1.0 / N)).reshape(cols, share, prior)
    for step in range(1, cols):
        peer = (col + step) % cols
        sent.append(to_col(corr.at[peer], corr_in.at[col], corr_send.at[step], corr_recv.at[col], peer))

    @pl.loop(EARLY, rows)
    def _(block):
        prepare(block)

    half = acc.shape[1] // 2

    def rays(source, columns):
        cur_high, cur_low = two_terms(current[source])
        both = product(jnp.concatenate([cur_high, cur_low], 0), a_high_t[source, :, columns], ROW_BY_COL)
        return both[:BS] + both[BS:] + product(cur_high, a_low_t[source, :, columns], ROW_BY_COL)

    acc[...] = rays(row, slice(None))

    @pl.loop(0, (rows - 1 - LAST) // GROUP)
    def _(group):
        sources = [row_before(row, far_first(group * GROUP + k + 1)) for k in range(GROUP)]
        for source in sources:
            arrive(current.at[source], cur_recv.at[source])
        total = acc[...]
        for source in sources:
            total += rays(source, slice(None))
        acc[...] = total

    sources = [row_before(row, step) for step in FAR_FIRST[rows - LAST - 1 :]]
    for source in sources:
        arrive(current.at[source], cur_recv.at[source])

    @pl.loop(0, 2)
    def _(part):
        columns = pl.ds(pl.multiple_of(part * half, half), half)
        total = acc[:, columns]
        for source in sources:
            total += rays(source, columns)
        parts[part, col] = total

        @pl.loop(1, cols)
        def _(step):
            to_col(parts.at[part, col], parts.at[part, col], part_send.at[part, step], part_recv.at[part, col], (col + step) % cols)

    total = corr[col]
    for step in range(1, cols):
        source = (col + cols - step) % cols
        arrive(corr_in.at[source], corr_recv.at[source])
        total += corr_in[source]
    corr_rows[row] = total
    for step in range(1, rows):
        peer = row_after(row, step)
        sent.append(to_row(corr_rows.at[row], corr_rows.at[row], crow_send.at[step], crow_recv.at[row], peer))

    halves = []
    for part in range(2):
        for step in range(1, cols):
            source = (col + cols - step) % cols
            arrive(parts.at[part, source], part_recv.at[part, source])
        total = parts[part, 0]
        for source in range(1, cols):
            total += parts[part, source]
        halves.append(total)
    projected = jnp.concatenate(halves, 1)

    pro_high, pro_low = two_terms(projected)
    pro_both = jnp.concatenate([pro_high, pro_low], 0)

    def block(peer):
        both = product(pro_both, a_high[peer], ROW_BY_COL)
        return both[:BS] + both[BS:] + product(pro_high, a_low[peer], ROW_BY_COL)

    @pl.loop(0, rows // GROUP_OUT)
    def _(group):
        steps = [group * GROUP_OUT + k + 1 for k in range(GROUP_OUT)]
        peers = [row_after(row, far_first(step)) for step in steps]
        for peer in peers:
            image_out[peer] = block(peer)
        for step, peer in zip(steps, peers):
            @pl.when(peer != row)
            def _():
                to_row(image_out.at[peer], image_in.at[row], image_send.at[step], image_recv.at[row], peer)

    for copy in sent:
        copy.wait_send()
    sent = []

    @pl.loop(1, cols)
    def _(step):
        for part in range(2):
            arrive(parts.at[part, col], part_send.at[part, step])

    total = jnp.zeros_like(corr_rows[0])
    for source in range(rows):
        @pl.when(source != row)
        def _():
            arrive(corr_rows.at[source], crow_recv.at[source])
        total += corr_rows[source]
    corr_whole[col] = total
    for step in range(1, cols):
        peer = (col + step) % cols
        sent.append(to_col(corr_whole.at[col], corr_whole.at[col], call_send.at[step], call_recv.at[col], peer))

    image = image_out[row]
    for step in FAR_FIRST:
        source = row_before(row, step)
        arrive(image_in.at[source], image_recv.at[source])
        image += image_in[source]

    own = basis[...]
    stat_cols[col] = exact(image, jnp.concatenate([own[: prior - BS], image], 0), ROW_BY_ROW) * (1.0 / N)
    for step in range(1, cols):
        peer = (col + step) % cols
        sent.append(to_col(stat_cols.at[col], stat_cols.at[col], scol_send.at[step], scol_recv.at[col], peer))

    square = exact(projected, projected, ROW_BY_ROW) * (1.0 / N)
    squares[row] = jnp.concatenate([square, jnp.zeros((BS, prior - BS), f32)], 1)
    for step in FAR_FIRST:
        peer = row_after(row, step)
        sent.append(to_row(squares.at[row], squares.at[row], square_send.at[step], square_recv.at[row], peer))

    for step in range(1, cols):
        source = (col + cols - step) % cols
        arrive(corr_whole.at[source], call_recv.at[source])
    correlation = corr_whole[...].reshape(prior, prior)
    at = lax.broadcasted_iota(jnp.int32, (prior, prior), 0)
    double = jnp.where(at == lax.broadcasted_iota(jnp.int32, (prior, prior), 1), 2.0, 0.0) - correlation
    inner = 2.0 * double - exact(exact(double, correlation, ROW_BY_COL), double, ROW_BY_COL)

    for step in range(1, cols):
        source = (col + cols - step) % cols
        arrive(stat_cols.at[source], scol_recv.at[source])
    total = stat_cols[0]
    for source in range(1, cols):
        total += stat_cols[source]
    stat_rows[row] = total
    last_sent = []
    for step in FAR_FIRST:
        peer = row_after(row, step)
        last_sent.append(to_row(stat_rows.at[row], stat_rows.at[row], srow_send.at[step], srow_recv.at[row], peer))
    for copy in sent:
        copy.wait_send()
    sent = []

    @pl.loop(1, rows)
    def _(step):
        arrive(image_out.at[row_after(row, far_first(step))], image_send.at[step])

    for step in range(1, rows):
        source = row_before(row, step)
        arrive(squares.at[source], square_recv.at[source])
    square = squares[0]
    for source in range(1, rows):
        square += squares[source]

    for step in FAR_FIRST:
        source = row_before(row, step)
        arrive(stat_rows.at[source], srow_recv.at[source])
    total = stat_rows[0]
    for source in range(1, rows):
        total += stat_rows[source]
    cross = jnp.concatenate([total[:, : prior - BS], square[:, :BS]], 1)
    self_gram = total[:, prior - BS :]
    coeffs = exact(cross, double, ROW_BY_ROW)
    gram = self_gram - exact(exact(cross, inner, ROW_BY_ROW), cross, ROW_BY_ROW)
    image -= exact(coeffs, own, ROW_BY_COL)
    coef_ref[...] = coeffs

    line = lax.broadcasted_iota(jnp.int32, (BS, BS), 0)
    lane = lax.broadcasted_iota(jnp.int32, (BS, BS), 1)
    below = lax.broadcasted_iota(jnp.int32, (BS, 1), 0)
    factor = jnp.zeros((BS, BS), f32)
    for j in range(BS):
        column = gram[:, j : j + 1]
        scale = lax.rsqrt(column[j : j + 1])
        column = column * scale
        gram_line = gram[j : j + 1] * scale
        image_line = image[j : j + 1] * scale
        factor = jnp.where((lane == j) & (line >= j), column, factor)
        part = jnp.where(below > j, column, 0.0)
        gram = gram - part * gram_line
        image = jnp.where(below == j, image_line, image - part * image_line)
    new_ref[...] = image
    factor_ref[...] = factor

    for copy in last_sent:
        copy.wait_send()


def local(rows, cols, projection, basis):
    rays, columns = projection.shape
    prior, width = basis.shape
    dma = pltpu.SemaphoreType.DMA
    call = pl.pallas_call(
        functools.partial(kernel, rows, cols),
        out_shape=(
            jax.ShapeDtypeStruct((BS, width), f32),
            jax.ShapeDtypeStruct((BS, prior), f32),
            jax.ShapeDtypeStruct((BS, BS), f32),
        ),
        in_specs=[pl.BlockSpec(memory_space=pltpu.HBM)] * 2,
        out_specs=[pl.BlockSpec(memory_space=pltpu.VMEM)] * 3,
        scratch_shapes=[
            pltpu.VMEM((DEPTH, rays, width), f32),
            pltpu.VMEM((rows, rays, width), bf16),
            pltpu.VMEM((rows, rays, width), bf16),
            pltpu.VMEM((rows, width, rays), bf16),
            pltpu.VMEM((rows, width, rays), bf16),
            pltpu.VMEM((prior, width), f32),
            pltpu.VMEM((rows, BS, width), f32),
            pltpu.VMEM((BS, rays), f32),
            pltpu.VMEM((2, cols, BS, rays // 2), f32),
            pltpu.VMEM((rows, BS, width), f32),
            pltpu.VMEM((rows, BS, width), f32),
            pltpu.VMEM((cols, prior // cols, prior), f32),
            pltpu.VMEM((cols, prior // cols, prior), f32),
            pltpu.VMEM((rows, prior // cols, prior), f32),
            pltpu.VMEM((cols, prior // cols, prior), f32),
            pltpu.VMEM((cols, BS, prior), f32),
            pltpu.VMEM((rows, BS, prior), f32),
            pltpu.VMEM((rows, BS, prior), f32),
            dma((DEPTH,)), dma,
            dma((rows,)), dma((rows,)),
            dma((2, cols)), dma((2, cols)),
            dma((rows,)), dma((rows,)),
            dma((cols,)), dma((cols,)), dma((rows,)), dma((rows,)), dma((cols,)), dma((cols,)),
            dma((cols,)), dma((cols,)), dma((rows,)), dma((rows,)), dma((rows,)), dma((rows,)),
        ],
        compiler_params=pltpu.CompilerParams(
            collective_id=0, has_side_effects=True, vmem_limit_bytes=55040 << 10
        ),
    )
    new_block, coefficients, factor = call(projection, basis)
    return new_block, coefficients.T, factor


def solution(mesh):
    placed = (P("rows", "cols"), P(None, ("cols", "rows")))
    return jax.shard_map(
        functools.partial(local, mesh.shape["rows"], mesh.shape["cols"]),
        mesh=mesh,
        in_specs=placed,
        out_specs=(P(None, ("cols", "rows")), P(), P()),
        check_vma=False,
    )
```

```python
import functools

import jax
import jax.numpy as jnp
from jax import lax
from jax.experimental import pallas as pl
from jax.experimental.pallas import tpu as pltpu
from jax.sharding import PartitionSpec as P

N = 65536
BS = 16
DEPTH = 6
EARLY = 3
LAST = 6
GROUP = 3
GROUP_OUT = 2
SIDE = 4
MESH = pl.DeviceIdType.MESH
FAR_FIRST = [10, 6, 9, 14, 11, 5, 15, 7, 13, 8, 2, 1, 12, 3, 4]
f32, bf16 = jnp.float32, jnp.bfloat16
ROW_BY_ROW = (((1,), (1,)), ((), ()))
ROW_BY_COL = (((1,), (0,)), ((), ()))


def product(left, right, dims):
    return lax.dot_general(left, right, dims, preferred_element_type=f32)


def exact(left, right, dims):
    return lax.dot_general(
        left, right, dims, precision=lax.Precision.HIGHEST, preferred_element_type=f32
    )


def two_terms(value):
    high = value.astype(bf16)
    return high, (value - high.astype(f32)).astype(bf16)


def row_after(row, step):
    x, y = row // SIDE, row % SIDE
    return (x + step // SIDE) % SIDE * SIDE + (y + step % SIDE) % SIDE


def row_before(row, step):
    x, y = row // SIDE, row % SIDE
    return (x + SIDE - step // SIDE) % SIDE * SIDE + (y + SIDE - step % SIDE) % SIDE


def far_first(step):
    place = 0
    for k, at in enumerate(FAR_FIRST):
        place = jnp.where(step == k + 1, at, place)
    return place


def arrive(buffer, sem):
    pltpu.make_async_copy(buffer, buffer, sem).wait()


def kernel(
    rows, cols, a_hbm, basis_hbm, new_ref, coef_ref, factor_ref,
    a_stage, a_high, a_low, a_high_t, a_low_t, basis, current, acc, parts,
    image_out, image_in, corr, corr_in, corr_rows, corr_whole, stat_cols, stat_rows, squares,
    a_sem, basis_sem, cur_send, cur_recv, part_send, part_recv,
    image_send, image_recv, corr_send, corr_recv, crow_send, crow_recv, call_send, call_recv,
    scol_send, scol_recv, srow_send, srow_recv, square_send, square_recv,
):
    row, col = lax.axis_index("rows"), lax.axis_index("cols")
    width = basis.shape[1]
    prior = basis.shape[0]

    def to_row(source, target, send, recv, peer):
        copy = pltpu.make_async_remote_copy(
            source, target, send, recv, device_id={"rows": peer}, device_id_type=MESH
        )
        copy.start()
        return copy

    def to_col(source, target, send, recv, peer):
        copy = pltpu.make_async_remote_copy(
            source, target, send, recv, device_id={"cols": peer}, device_id_type=MESH
        )
        copy.start()
        return copy

    sent = []
    barrier = pltpu.get_barrier_semaphore()
    for step in FAR_FIRST:
        pl.semaphore_signal(barrier, inc=1, device_id={"rows": row_after(row, step)}, device_id_type=MESH)
    for step in range(1, cols):
        pl.semaphore_signal(barrier, inc=1, device_id={"cols": (col + step) % cols}, device_id_type=MESH)

    last = basis_hbm.at[pl.ds(prior - BS, BS)]
    pltpu.make_async_copy(last, current.at[row], cur_recv.at[row]).start()
    load_basis = pltpu.make_async_copy(basis_hbm, basis, basis_sem)
    load_basis.start()

    depth = a_stage.shape[0]

    def fetch(block):
        columns = pl.ds(pl.multiple_of(block * width, width), width)
        slot = block % depth
        return pltpu.make_async_copy(a_hbm.at[:, columns], a_stage.at[slot], a_sem.at[slot])

    def prepare(block):
        fetch(block).wait()
        plain = a_stage[block % depth]
        turned = plain.T
        high, low = two_terms(plain)
        a_high[block] = high
        a_low[block] = low
        high, low = two_terms(turned)
        a_high_t[block] = high
        a_low_t[block] = low

        @pl.when(block + depth < rows)
        def _():
            fetch(block + depth).start()

    for block in range(depth):
        fetch(block).start(priority=1)

    @pl.loop(0, EARLY)
    def _(block):
        prepare(block)

    arrive(current.at[row], cur_recv.at[row])
    pl.semaphore_wait(barrier, rows + cols - 2)

    for step in FAR_FIRST:
        peer = row_after(row, step)
        sent.append(to_row(current.at[row], current.at[row], cur_send.at[step], cur_recv.at[row], peer))

    load_basis.wait()
    share = prior // cols
    corr[...] = (exact(basis[...], basis[...], ROW_BY_ROW) * (1.0 / N)).reshape(cols, share, prior)
    for step in range(1, cols):
        peer = (col + step) % cols
        sent.append(to_col(corr.at[peer], corr_in.at[col], corr_send.at[step], corr_recv.at[col], peer))

    @pl.loop(EARLY, rows)
    def _(block):
        prepare(block)

    half = acc.shape[1] // 2

    def rays(source, columns):
        cur_high, cur_low = two_terms(current[source])
        both = product(jnp.concatenate([cur_high, cur_low], 0), a_high_t[source, :, columns], ROW_BY_COL)
        return both[:BS] + both[BS:] + product(cur_high, a_low_t[source, :, columns], ROW_BY_COL)

    acc[...] = rays(row, slice(None))

    @pl.loop(0, (rows - 1 - LAST) // GROUP)
    def _(group):
        sources = [row_before(row, far_first(group * GROUP + k + 1)) for k in range(GROUP)]
        for source in sources:
            arrive(current.at[source], cur_recv.at[source])
        total = acc[...]
        for source in sources:
            total += rays(source, slice(None))
        acc[...] = total

    sources = [row_before(row, step) for step in FAR_FIRST[rows - LAST - 1 :]]
    for source in sources:
        arrive(current.at[source], cur_recv.at[source])

    @pl.loop(0, 2)
    def _(part):
        columns = pl.ds(pl.multiple_of(part * half, half), half)
        total = acc[:, columns]
        for source in sources:
            total += rays(source, columns)
        parts[part, col] = total

        @pl.loop(1, cols)
        def _(step):
            to_col(parts.at[part, col], parts.at[part, col], part_send.at[part, step], part_recv.at[part, col], (col + step) % cols)

    total = corr[col]
    for step in range(1, cols):
        source = (col + cols - step) % cols
        arrive(corr_in.at[source], corr_recv.at[source])
        total += corr_in[source]
    corr_rows[row] = total
    for step in range(1, rows):
        peer = row_after(row, step)
        sent.append(to_row(corr_rows.at[row], corr_rows.at[row], crow_send.at[step], crow_recv.at[row], peer))

    halves = []
    for part in range(2):
        for step in range(1, cols):
            source = (col + cols - step) % cols
            arrive(parts.at[part, source], part_recv.at[part, source])
        total = parts[part, 0]
        for source in range(1, cols):
            total += parts[part, source]
        halves.append(total)
    projected = jnp.concatenate(halves, 1)

    pro_high, pro_low = two_terms(projected)
    pro_both = jnp.concatenate([pro_high, pro_low], 0)

    def block(peer):
        both = product(pro_both, a_high[peer], ROW_BY_COL)
        return both[:BS] + both[BS:] + product(pro_high, a_low[peer], ROW_BY_COL)

    @pl.loop(0, rows // GROUP_OUT)
    def _(group):
        steps = [group * GROUP_OUT + k + 1 for k in range(GROUP_OUT)]
        peers = [row_after(row, far_first(step)) for step in steps]
        for peer in peers:
            image_out[peer] = block(peer)
        for step, peer in zip(steps, peers):
            @pl.when(peer != row)
            def _():
                to_row(image_out.at[peer], image_in.at[row], image_send.at[step], image_recv.at[row], peer)

    for copy in sent:
        copy.wait_send()
    sent = []

    @pl.loop(1, cols)
    def _(step):
        for part in range(2):
            arrive(parts.at[part, col], part_send.at[part, step])

    total = jnp.zeros_like(corr_rows[0])
    for source in range(rows):
        @pl.when(source != row)
        def _():
            arrive(corr_rows.at[source], crow_recv.at[source])
        total += corr_rows[source]
    corr_whole[col] = total
    for step in range(1, cols):
        peer = (col + step) % cols
        sent.append(to_col(corr_whole.at[col], corr_whole.at[col], call_send.at[step], call_recv.at[col], peer))

    image = image_out[row]
    for step in FAR_FIRST:
        source = row_before(row, step)
        arrive(image_in.at[source], image_recv.at[source])
        image += image_in[source]

    own = basis[...]
    stat_cols[col] = exact(image, jnp.concatenate([own[: prior - BS], image], 0), ROW_BY_ROW) * (1.0 / N)
    for step in range(1, cols):
        peer = (col + step) % cols
        sent.append(to_col(stat_cols.at[col], stat_cols.at[col], scol_send.at[step], scol_recv.at[col], peer))

    square = exact(projected, projected, ROW_BY_ROW) * (1.0 / N)
    squares[row] = jnp.concatenate([square, jnp.zeros((BS, prior - BS), f32)], 1)
    for step in FAR_FIRST:
        peer = row_after(row, step)
        sent.append(to_row(squares.at[row], squares.at[row], square_send.at[step], square_recv.at[row], peer))

    for step in range(1, cols):
        source = (col + cols - step) % cols
        arrive(corr_whole.at[source], call_recv.at[source])
    correlation = corr_whole[...].reshape(prior, prior)
    at = lax.broadcasted_iota(jnp.int32, (prior, prior), 0)
    double = jnp.where(at == lax.broadcasted_iota(jnp.int32, (prior, prior), 1), 2.0, 0.0) - correlation
    inner = 2.0 * double - exact(exact(double, correlation, ROW_BY_COL), double, ROW_BY_COL)

    for step in range(1, cols):
        source = (col + cols - step) % cols
        arrive(stat_cols.at[source], scol_recv.at[source])
    total = stat_cols[0]
    for source in range(1, cols):
        total += stat_cols[source]
    stat_rows[row] = total
    last_sent = []
    for step in FAR_FIRST:
        peer = row_after(row, step)
        last_sent.append(to_row(stat_rows.at[row], stat_rows.at[row], srow_send.at[step], srow_recv.at[row], peer))
    for copy in sent:
        copy.wait_send()
    sent = []

    @pl.loop(1, rows)
    def _(step):
        arrive(image_out.at[row_after(row, far_first(step))], image_send.at[step])

    for step in range(1, rows):
        source = row_before(row, step)
        arrive(squares.at[source], square_recv.at[source])
    square = squares[0]
    for source in range(1, rows):
        square += squares[source]

    for step in FAR_FIRST:
        source = row_before(row, step)
        arrive(stat_rows.at[source], srow_recv.at[source])
    total = stat_rows[0]
    for source in range(1, rows):
        total += stat_rows[source]
    cross = jnp.concatenate([total[:, : prior - BS], square[:, :BS]], 1)
    self_gram = total[:, prior - BS :]
    coeffs = exact(cross, double, ROW_BY_ROW)
    gram = self_gram - exact(exact(cross, inner, ROW_BY_ROW), cross, ROW_BY_ROW)
    image -= exact(coeffs, own, ROW_BY_COL)
    coef_ref[...] = coeffs

    line = lax.broadcasted_iota(jnp.int32, (BS, BS), 0)
    lane = lax.broadcasted_iota(jnp.int32, (BS, BS), 1)
    below = lax.broadcasted_iota(jnp.int32, (BS, 1), 0)
    factor = jnp.zeros((BS, BS), f32)
    for j in range(BS):
        column = gram[:, j : j + 1]
        scale = lax.rsqrt(column[j : j + 1])
        column = column * scale
        gram_line = gram[j : j + 1] * scale
        image_line = image[j : j + 1] * scale
        factor = jnp.where((lane == j) & (line >= j), column, factor)
        part = jnp.where(below > j, column, 0.0)
        gram = gram - part * gram_line
        image = jnp.where(below == j, image_line, image - part * image_line)
    new_ref[...] = image
    factor_ref[...] = factor

    for copy in last_sent:
        copy.wait_send()


def local(rows, cols, projection, basis):
    rays, columns = projection.shape
    prior, width = basis.shape
    dma = pltpu.SemaphoreType.DMA
    call = pl.pallas_call(
        functools.partial(kernel, rows, cols),
        out_shape=(
            jax.ShapeDtypeStruct((BS, width), f32),
            jax.ShapeDtypeStruct((BS, prior), f32),
            jax.ShapeDtypeStruct((BS, BS), f32),
        ),
        in_specs=[pl.BlockSpec(memory_space=pltpu.HBM)] * 2,
        out_specs=[pl.BlockSpec(memory_space=pltpu.VMEM)] * 3,
        scratch_shapes=[
            pltpu.VMEM((DEPTH, rays, width), f32),
            pltpu.VMEM((rows, rays, width), bf16),
            pltpu.VMEM((rows, rays, width), bf16),
            pltpu.VMEM((rows, width, rays), bf16),
            pltpu.VMEM((rows, width, rays), bf16),
            pltpu.VMEM((prior, width), f32),
            pltpu.VMEM((rows, BS, width), f32),
            pltpu.VMEM((BS, rays), f32),
            pltpu.VMEM((2, cols, BS, rays // 2), f32),
            pltpu.VMEM((rows, BS, width), f32),
            pltpu.VMEM((rows, BS, width), f32),
            pltpu.VMEM((cols, prior // cols, prior), f32),
            pltpu.VMEM((cols, prior // cols, prior), f32),
            pltpu.VMEM((rows, prior // cols, prior), f32),
            pltpu.VMEM((cols, prior // cols, prior), f32),
            pltpu.VMEM((cols, BS, prior), f32),
            pltpu.VMEM((rows, BS, prior), f32),
            pltpu.VMEM((rows, BS, prior), f32),
            dma((DEPTH,)), dma,
            dma((rows,)), dma((rows,)),
            dma((2, cols)), dma((2, cols)),
            dma((rows,)), dma((rows,)),
            dma((cols,)), dma((cols,)), dma((rows,)), dma((rows,)), dma((cols,)), dma((cols,)),
            dma((cols,)), dma((cols,)), dma((rows,)), dma((rows,)), dma((rows,)), dma((rows,)),
        ],
        compiler_params=pltpu.CompilerParams(
            collective_id=0, has_side_effects=True, vmem_limit_bytes=55040 << 10
        ),
    )
    new_block, coefficients, factor = call(projection, basis)
    return new_block, coefficients.T, factor


def solution(mesh):
    placed = (P("rows", "cols"), P(None, ("cols", "rows")))
    return jax.shard_map(
        functools.partial(local, mesh.shape["rows"], mesh.shape["cols"]),
        mesh=mesh,
        in_specs=placed,
        out_specs=(P(None, ("cols", "rows")), P(), P()),
        check_vma=False,
    )
```

```python
import functools

import jax
import jax.numpy as jnp
from jax import lax
from jax.experimental import pallas as pl
from jax.experimental.pallas import tpu as pltpu
from jax.sharding import PartitionSpec as P

N = 65536
BS = 16
DEPTH = 4
EARLY = 3
LAST = 9
GROUP = 3
GROUP_OUT = 2
SIDE = 4
MESH = pl.DeviceIdType.MESH
FAR_FIRST = [10, 6, 9, 14, 11, 5, 7, 13, 15, 8, 2, 1, 3, 4, 12]
f32, bf16 = jnp.float32, jnp.bfloat16
ROW_BY_ROW = (((1,), (1,)), ((), ()))
ROW_BY_COL = (((1,), (0,)), ((), ()))


def product(left, right, dims):
    return lax.dot_general(left, right, dims, preferred_element_type=f32)


def exact(left, right, dims):
    return lax.dot_general(
        left, right, dims, precision=lax.Precision.HIGHEST, preferred_element_type=f32
    )


def two_terms(value):
    high = value.astype(bf16)
    return high, (value - high.astype(f32)).astype(bf16)


def row_after(row, step):
    x, y = row // SIDE, row % SIDE
    return (x + step // SIDE) % SIDE * SIDE + (y + step % SIDE) % SIDE


def row_before(row, step):
    x, y = row // SIDE, row % SIDE
    return (x + SIDE - step // SIDE) % SIDE * SIDE + (y + SIDE - step % SIDE) % SIDE


def far_first(step):
    place = 0
    for k, at in enumerate(FAR_FIRST):
        place = jnp.where(step == k + 1, at, place)
    return place


def arrive(buffer, sem):
    pltpu.make_async_copy(buffer, buffer, sem).wait()


def kernel(
    rows, cols, a_hbm, basis_hbm, new_ref, coef_ref, factor_ref,
    a_stage, a_high, a_low, a_high_t, a_low_t, basis, current, acc, parts,
    image_out, image_in, corr, corr_in, corr_rows, corr_whole, stat_cols, stat_rows, squares,
    a_sem, basis_sem, cur_send, cur_recv, part_send, part_recv,
    image_send, image_recv, corr_send, corr_recv, crow_send, crow_recv, call_send, call_recv,
    scol_send, scol_recv, srow_send, srow_recv, square_send, square_recv,
):
    row, col = lax.axis_index("rows"), lax.axis_index("cols")
    width = basis.shape[1]
    prior = basis.shape[0]

    def to_row(source, target, send, recv, peer):
        copy = pltpu.make_async_remote_copy(
            source, target, send, recv, device_id={"rows": peer}, device_id_type=MESH
        )
        copy.start()
        return copy

    def to_col(source, target, send, recv, peer):
        copy = pltpu.make_async_remote_copy(
            source, target, send, recv, device_id={"cols": peer}, device_id_type=MESH
        )
        copy.start()
        return copy

    sent = []
    barrier = pltpu.get_barrier_semaphore()
    for step in FAR_FIRST:
        pl.semaphore_signal(barrier, inc=1, device_id={"rows": row_after(row, step)}, device_id_type=MESH)
    for step in range(1, cols):
        pl.semaphore_signal(barrier, inc=1, device_id={"cols": (col + step) % cols}, device_id_type=MESH)

    last = basis_hbm.at[pl.ds(prior - BS, BS)]
    pltpu.make_async_copy(last, current.at[row], cur_recv.at[row]).start()
    load_basis = pltpu.make_async_copy(basis_hbm, basis, basis_sem)
    load_basis.start()

    depth = a_stage.shape[0]

    def fetch(block):
        columns = pl.ds(pl.multiple_of(block * width, width), width)
        slot = block % depth
        return pltpu.make_async_copy(a_hbm.at[:, columns], a_stage.at[slot], a_sem.at[slot])

    def prepare(block):
        fetch(block).wait()
        plain = a_stage[block % depth]
        turned = plain.T
        high, low = two_terms(plain)
        a_high[block] = high
        a_low[block] = low
        high, low = two_terms(turned)
        a_high_t[block] = high
        a_low_t[block] = low

        @pl.when(block + depth < rows)
        def _():
            fetch(block + depth).start()

    for block in range(depth):
        fetch(block).start()

    @pl.loop(0, EARLY)
    def _(block):
        prepare(block)

    arrive(current.at[row], cur_recv.at[row])
    pl.semaphore_wait(barrier, rows + cols - 2)

    for step in FAR_FIRST:
        peer = row_after(row, step)
        sent.append(to_row(current.at[row], current.at[row], cur_send.at[step], cur_recv.at[row], peer))

    load_basis.wait()
    share = prior // cols
    corr[...] = (exact(basis[...], basis[...], ROW_BY_ROW) * (1.0 / N)).reshape(cols, share, prior)
    for step in range(1, cols):
        peer = (col + step) % cols
        sent.append(to_col(corr.at[peer], corr_in.at[col], corr_send.at[step], corr_recv.at[col], peer))

    @pl.loop(EARLY, rows)
    def _(block):
        prepare(block)

    half = acc.shape[1] // 2

    def rays(source, columns):
        cur_high, cur_low = two_terms(current[source])
        both = product(jnp.concatenate([cur_high, cur_low], 0), a_high_t[source, :, columns], ROW_BY_COL)
        return both[:BS] + both[BS:] + product(cur_high, a_low_t[source, :, columns], ROW_BY_COL)

    acc[...] = rays(row, slice(None))

    @pl.loop(0, (rows - 1 - LAST) // GROUP)
    def _(group):
        sources = [row_before(row, far_first(group * GROUP + k + 1)) for k in range(GROUP)]
        for source in sources:
            arrive(current.at[source], cur_recv.at[source])
        total = acc[...]
        for source in sources:
            total += rays(source, slice(None))
        acc[...] = total

    sources = [row_before(row, step) for step in FAR_FIRST[rows - LAST - 1 :]]
    for source in sources:
        arrive(current.at[source], cur_recv.at[source])

    @pl.loop(0, 2)
    def _(part):
        columns = pl.ds(pl.multiple_of(part * half, half), half)
        total = acc[:, columns]
        for source in sources:
            total += rays(source, columns)
        parts[part, col] = total

        @pl.loop(1, cols)
        def _(step):
            to_col(parts.at[part, col], parts.at[part, col], part_send.at[part, step], part_recv.at[part, col], (col + step) % cols)

    total = corr[col]
    for step in range(1, cols):
        source = (col + cols - step) % cols
        arrive(corr_in.at[source], corr_recv.at[source])
        total += corr_in[source]
    corr_rows[row] = total
    for step in range(1, rows):
        peer = row_after(row, step)
        sent.append(to_row(corr_rows.at[row], corr_rows.at[row], crow_send.at[step], crow_recv.at[row], peer))

    halves = []
    for part in range(2):
        for step in range(1, cols):
            source = (col + cols - step) % cols
            arrive(parts.at[part, source], part_recv.at[part, source])
        total = parts[part, 0]
        for source in range(1, cols):
            total += parts[part, source]
        halves.append(total)
    projected = jnp.concatenate(halves, 1)

    pro_high, pro_low = two_terms(projected)
    pro_both = jnp.concatenate([pro_high, pro_low], 0)

    def block(peer):
        both = product(pro_both, a_high[peer], ROW_BY_COL)
        return both[:BS] + both[BS:] + product(pro_high, a_low[peer], ROW_BY_COL)

    @pl.loop(0, rows // GROUP_OUT)
    def _(group):
        steps = [group * GROUP_OUT + k + 1 for k in range(GROUP_OUT)]
        peers = [row_after(row, far_first(step)) for step in steps]
        for peer in peers:
            image_out[peer] = block(peer)
        for step, peer in zip(steps, peers):
            @pl.when(peer != row)
            def _():
                to_row(image_out.at[peer], image_in.at[row], image_send.at[step], image_recv.at[row], peer)

    for copy in sent:
        copy.wait_send()
    sent = []

    @pl.loop(1, cols)
    def _(step):
        for part in range(2):
            arrive(parts.at[part, col], part_send.at[part, step])

    total = jnp.zeros_like(corr_rows[0])
    for source in range(rows):
        @pl.when(source != row)
        def _():
            arrive(corr_rows.at[source], crow_recv.at[source])
        total += corr_rows[source]
    corr_whole[col] = total
    for step in range(1, cols):
        peer = (col + step) % cols
        sent.append(to_col(corr_whole.at[col], corr_whole.at[col], call_send.at[step], call_recv.at[col], peer))

    image = image_out[row]
    for step in FAR_FIRST:
        source = row_before(row, step)
        arrive(image_in.at[source], image_recv.at[source])
        image += image_in[source]

    own = basis[...]
    stat_cols[col] = exact(image, jnp.concatenate([own[: prior - BS], image], 0), ROW_BY_ROW) * (1.0 / N)
    for step in range(1, cols):
        peer = (col + step) % cols
        sent.append(to_col(stat_cols.at[col], stat_cols.at[col], scol_send.at[step], scol_recv.at[col], peer))

    square = exact(projected, projected, ROW_BY_ROW) * (1.0 / N)
    squares[row] = jnp.concatenate([square, jnp.zeros((BS, prior - BS), f32)], 1)
    for step in FAR_FIRST:
        peer = row_after(row, step)
        sent.append(to_row(squares.at[row], squares.at[row], square_send.at[step], square_recv.at[row], peer))

    for step in range(1, cols):
        source = (col + cols - step) % cols
        arrive(corr_whole.at[source], call_recv.at[source])
    correlation = corr_whole[...].reshape(prior, prior)
    at = lax.broadcasted_iota(jnp.int32, (prior, prior), 0)
    double = jnp.where(at == lax.broadcasted_iota(jnp.int32, (prior, prior), 1), 2.0, 0.0) - correlation
    inner = 2.0 * double - exact(exact(double, correlation, ROW_BY_COL), double, ROW_BY_COL)

    for step in range(1, cols):
        source = (col + cols - step) % cols
        arrive(stat_cols.at[source], scol_recv.at[source])
    total = stat_cols[0]
    for source in range(1, cols):
        total += stat_cols[source]
    stat_rows[row] = total
    last_sent = []
    for step in FAR_FIRST:
        peer = row_after(row, step)
        last_sent.append(to_row(stat_rows.at[row], stat_rows.at[row], srow_send.at[step], srow_recv.at[row], peer))
    for copy in sent:
        copy.wait_send()
    sent = []

    @pl.loop(1, rows)
    def _(step):
        arrive(image_out.at[row_after(row, far_first(step))], image_send.at[step])

    for step in range(1, rows):
        source = row_before(row, step)
        arrive(squares.at[source], square_recv.at[source])
    square = squares[0]
    for source in range(1, rows):
        square += squares[source]

    for step in FAR_FIRST:
        source = row_before(row, step)
        arrive(stat_rows.at[source], srow_recv.at[source])
    total = stat_rows[0]
    for source in range(1, rows):
        total += stat_rows[source]
    cross = jnp.concatenate([total[:, : prior - BS], square[:, :BS]], 1)
    self_gram = total[:, prior - BS :]
    coeffs = exact(cross, double, ROW_BY_ROW)
    gram = self_gram - exact(exact(cross, inner, ROW_BY_ROW), cross, ROW_BY_ROW)
    image -= exact(coeffs, own, ROW_BY_COL)
    coef_ref[...] = coeffs

    line = lax.broadcasted_iota(jnp.int32, (BS, BS), 0)
    lane = lax.broadcasted_iota(jnp.int32, (BS, BS), 1)
    below = lax.broadcasted_iota(jnp.int32, (BS, 1), 0)
    factor = jnp.zeros((BS, BS), f32)
    for j in range(BS):
        column = gram[:, j : j + 1]
        scale = lax.rsqrt(column[j : j + 1])
        column = column * scale
        gram_line = gram[j : j + 1] * scale
        image_line = image[j : j + 1] * scale
        factor = jnp.where((lane == j) & (line >= j), column, factor)
        part = jnp.where(below > j, column, 0.0)
        gram = gram - part * gram_line
        image = jnp.where(below == j, image_line, image - part * image_line)
    new_ref[...] = image
    factor_ref[...] = factor

    for copy in last_sent:
        copy.wait_send()


def local(rows, cols, projection, basis):
    rays, columns = projection.shape
    prior, width = basis.shape
    dma = pltpu.SemaphoreType.DMA
    call = pl.pallas_call(
        functools.partial(kernel, rows, cols),
        out_shape=(
            jax.ShapeDtypeStruct((BS, width), f32),
            jax.ShapeDtypeStruct((BS, prior), f32),
            jax.ShapeDtypeStruct((BS, BS), f32),
        ),
        in_specs=[pl.BlockSpec(memory_space=pltpu.HBM)] * 2,
        out_specs=[pl.BlockSpec(memory_space=pltpu.VMEM)] * 3,
        scratch_shapes=[
            pltpu.VMEM((DEPTH, rays, width), f32),
            pltpu.VMEM((rows, rays, width), bf16),
            pltpu.VMEM((rows, rays, width), bf16),
            pltpu.VMEM((rows, width, rays), bf16),
            pltpu.VMEM((rows, width, rays), bf16),
            pltpu.VMEM((prior, width), f32),
            pltpu.VMEM((rows, BS, width), f32),
            pltpu.VMEM((BS, rays), f32),
            pltpu.VMEM((2, cols, BS, rays // 2), f32),
            pltpu.VMEM((rows, BS, width), f32),
            pltpu.VMEM((rows, BS, width), f32),
            pltpu.VMEM((cols, prior // cols, prior), f32),
            pltpu.VMEM((cols, prior // cols, prior), f32),
            pltpu.VMEM((rows, prior // cols, prior), f32),
            pltpu.VMEM((cols, prior // cols, prior), f32),
            pltpu.VMEM((cols, BS, prior), f32),
            pltpu.VMEM((rows, BS, prior), f32),
            pltpu.VMEM((rows, BS, prior), f32),
            dma((DEPTH,)), dma,
            dma((rows,)), dma((rows,)),
            dma((2, cols)), dma((2, cols)),
            dma((rows,)), dma((rows,)),
            dma((cols,)), dma((cols,)), dma((rows,)), dma((rows,)), dma((cols,)), dma((cols,)),
            dma((cols,)), dma((cols,)), dma((rows,)), dma((rows,)), dma((rows,)), dma((rows,)),
        ],
        compiler_params=pltpu.CompilerParams(
            collective_id=0, has_side_effects=True, vmem_limit_bytes=55040 << 10
        ),
    )
    new_block, coefficients, factor = call(projection, basis)
    return new_block, coefficients.T, factor


def solution(mesh):
    placed = (P("rows", "cols"), P(None, ("cols", "rows")))
    return jax.shard_map(
        functools.partial(local, mesh.shape["rows"], mesh.shape["cols"]),
        mesh=mesh,
        in_specs=placed,
        out_specs=(P(None, ("cols", "rows")), P(), P()),
        check_vma=False,
    )
```

```python
import functools

import jax
import jax.numpy as jnp
from jax import lax
from jax.experimental import pallas as pl
from jax.experimental.pallas import tpu as pltpu
from jax.sharding import PartitionSpec as P

N = 65536
BS = 16
DEPTH = 6
EARLY = 3
LAST = 6
GROUP = 3
GROUP_OUT = 2
SIDE = 4
MESH = pl.DeviceIdType.MESH
FAR_FIRST = [10, 6, 9, 14, 11, 8, 2, 5, 7, 13, 15, 1, 3, 4, 12]
f32, bf16 = jnp.float32, jnp.bfloat16
ROW_BY_ROW = (((1,), (1,)), ((), ()))
ROW_BY_COL = (((1,), (0,)), ((), ()))


def product(left, right, dims):
    return lax.dot_general(left, right, dims, preferred_element_type=f32)


def exact(left, right, dims):
    return lax.dot_general(
        left, right, dims, precision=lax.Precision.HIGHEST, preferred_element_type=f32
    )


def two_terms(value):
    high = value.astype(bf16)
    return high, (value - high.astype(f32)).astype(bf16)


def row_after(row, step):
    x, y = row // SIDE, row % SIDE
    return (x + step // SIDE) % SIDE * SIDE + (y + step % SIDE) % SIDE


def row_before(row, step):
    x, y = row // SIDE, row % SIDE
    return (x + SIDE - step // SIDE) % SIDE * SIDE + (y + SIDE - step % SIDE) % SIDE


def far_first(step):
    place = 0
    for k, at in enumerate(FAR_FIRST):
        place = jnp.where(step == k + 1, at, place)
    return place


def arrive(buffer, sem):
    pltpu.make_async_copy(buffer, buffer, sem).wait()


def kernel(
    rows, cols, a_hbm, basis_hbm, new_ref, coef_ref, factor_ref,
    a_stage, a_high, a_low, a_high_t, a_low_t, basis, current, acc, parts,
    image_out, image_in, corr, corr_in, corr_rows, corr_whole, stat_cols, stat_rows, squares,
    a_sem, basis_sem, cur_send, cur_recv, part_send, part_recv,
    image_send, image_recv, corr_send, corr_recv, crow_send, crow_recv, call_send, call_recv,
    scol_send, scol_recv, srow_send, srow_recv, square_send, square_recv,
):
    row, col = lax.axis_index("rows"), lax.axis_index("cols")
    width = basis.shape[1]
    prior = basis.shape[0]

    def to_row(source, target, send, recv, peer):
        copy = pltpu.make_async_remote_copy(
            source, target, send, recv, device_id={"rows": peer}, device_id_type=MESH
        )
        copy.start()
        return copy

    def to_col(source, target, send, recv, peer):
        copy = pltpu.make_async_remote_copy(
            source, target, send, recv, device_id={"cols": peer}, device_id_type=MESH
        )
        copy.start()
        return copy

    sent = []
    barrier = pltpu.get_barrier_semaphore()
    for step in FAR_FIRST:
        pl.semaphore_signal(barrier, inc=1, device_id={"rows": row_after(row, step)}, device_id_type=MESH)
    for step in range(1, cols):
        pl.semaphore_signal(barrier, inc=1, device_id={"cols": (col + step) % cols}, device_id_type=MESH)

    last = basis_hbm.at[pl.ds(prior - BS, BS)]
    pltpu.make_async_copy(last, current.at[row], cur_recv.at[row]).start()
    load_basis = pltpu.make_async_copy(basis_hbm, basis, basis_sem)
    load_basis.start()

    depth = a_stage.shape[0]

    def fetch(block):
        columns = pl.ds(pl.multiple_of(block * width, width), width)
        slot = block % depth
        return pltpu.make_async_copy(a_hbm.at[:, columns], a_stage.at[slot], a_sem.at[slot])

    def prepare(block):
        fetch(block).wait()
        plain = a_stage[block % depth]
        turned = plain.T
        high, low = two_terms(plain)
        a_high[block] = high
        a_low[block] = low
        high, low = two_terms(turned)
        a_high_t[block] = high
        a_low_t[block] = low

        @pl.when(block + depth < rows)
        def _():
            fetch(block + depth).start()

    for block in range(depth):
        fetch(block).start()

    @pl.loop(0, EARLY)
    def _(block):
        prepare(block)

    arrive(current.at[row], cur_recv.at[row])
    pl.semaphore_wait(barrier, rows + cols - 2)

    for step in FAR_FIRST:
        peer = row_after(row, step)
        sent.append(to_row(current.at[row], current.at[row], cur_send.at[step], cur_recv.at[row], peer))

    load_basis.wait()
    share = prior // cols
    corr[...] = (exact(basis[...], basis[...], ROW_BY_ROW) * (1.0 / N)).reshape(cols, share, prior)
    for step in range(1, cols):
        peer = (col + step) % cols
        sent.append(to_col(corr.at[peer], corr_in.at[col], corr_send.at[step], corr_recv.at[col], peer))

    @pl.loop(EARLY, rows)
    def _(block):
        prepare(block)

    half = acc.shape[1] // 2

    def rays(source, columns):
        cur_high, cur_low = two_terms(current[source])
        both = product(jnp.concatenate([cur_high, cur_low], 0), a_high_t[source, :, columns], ROW_BY_COL)
        return both[:BS] + both[BS:] + product(cur_high, a_low_t[source, :, columns], ROW_BY_COL)

    acc[...] = rays(row, slice(None))

    @pl.loop(0, (rows - 1 - LAST) // GROUP)
    def _(group):
        sources = [row_before(row, far_first(group * GROUP + k + 1)) for k in range(GROUP)]
        for source in sources:
            arrive(current.at[source], cur_recv.at[source])
        total = acc[...]
        for source in sources:
            total += rays(source, slice(None))
        acc[...] = total

    sources = [row_before(row, step) for step in FAR_FIRST[rows - LAST - 1 :]]
    for source in sources:
        arrive(current.at[source], cur_recv.at[source])

    @pl.loop(0, 2)
    def _(part):
        columns = pl.ds(pl.multiple_of(part * half, half), half)
        total = acc[:, columns]
        for source in sources:
            total += rays(source, columns)
        parts[part, col] = total

        @pl.loop(1, cols)
        def _(step):
            to_col(parts.at[part, col], parts.at[part, col], part_send.at[part, step], part_recv.at[part, col], (col + step) % cols)

    total = corr[col]
    for step in range(1, cols):
        source = (col + cols - step) % cols
        arrive(corr_in.at[source], corr_recv.at[source])
        total += corr_in[source]
    corr_rows[row] = total
    for step in range(1, rows):
        peer = row_after(row, step)
        sent.append(to_row(corr_rows.at[row], corr_rows.at[row], crow_send.at[step], crow_recv.at[row], peer))

    halves = []
    for part in range(2):
        for step in range(1, cols):
            source = (col + cols - step) % cols
            arrive(parts.at[part, source], part_recv.at[part, source])
        total = parts[part, 0]
        for source in range(1, cols):
            total += parts[part, source]
        halves.append(total)
    projected = jnp.concatenate(halves, 1)

    pro_high, pro_low = two_terms(projected)
    pro_both = jnp.concatenate([pro_high, pro_low], 0)

    def block(peer):
        both = product(pro_both, a_high[peer], ROW_BY_COL)
        return both[:BS] + both[BS:] + product(pro_high, a_low[peer], ROW_BY_COL)

    @pl.loop(0, rows // GROUP_OUT)
    def _(group):
        steps = [group * GROUP_OUT + k + 1 for k in range(GROUP_OUT)]
        peers = [row_after(row, far_first(step)) for step in steps]
        for peer in peers:
            image_out[peer] = block(peer)
        for step, peer in zip(steps, peers):
            @pl.when(peer != row)
            def _():
                to_row(image_out.at[peer], image_in.at[row], image_send.at[step], image_recv.at[row], peer)

    for copy in sent:
        copy.wait_send()
    sent = []

    @pl.loop(1, cols)
    def _(step):
        for part in range(2):
            arrive(parts.at[part, col], part_send.at[part, step])

    total = jnp.zeros_like(corr_rows[0])
    for source in range(rows):
        @pl.when(source != row)
        def _():
            arrive(corr_rows.at[source], crow_recv.at[source])
        total += corr_rows[source]
    corr_whole[col] = total
    for step in range(1, cols):
        peer = (col + step) % cols
        sent.append(to_col(corr_whole.at[col], corr_whole.at[col], call_send.at[step], call_recv.at[col], peer))

    image = image_out[row]
    for step in FAR_FIRST:
        source = row_before(row, step)
        arrive(image_in.at[source], image_recv.at[source])
        image += image_in[source]

    own = basis[...]
    stat_cols[col] = exact(image, jnp.concatenate([own[: prior - BS], image], 0), ROW_BY_ROW) * (1.0 / N)
    for step in range(1, cols):
        peer = (col + step) % cols
        sent.append(to_col(stat_cols.at[col], stat_cols.at[col], scol_send.at[step], scol_recv.at[col], peer))

    square = exact(projected, projected, ROW_BY_ROW) * (1.0 / N)
    squares[row] = jnp.concatenate([square, jnp.zeros((BS, prior - BS), f32)], 1)
    for step in FAR_FIRST:
        peer = row_after(row, step)
        sent.append(to_row(squares.at[row], squares.at[row], square_send.at[step], square_recv.at[row], peer))

    for step in range(1, cols):
        source = (col + cols - step) % cols
        arrive(corr_whole.at[source], call_recv.at[source])
    correlation = corr_whole[...].reshape(prior, prior)
    at = lax.broadcasted_iota(jnp.int32, (prior, prior), 0)
    double = jnp.where(at == lax.broadcasted_iota(jnp.int32, (prior, prior), 1), 2.0, 0.0) - correlation
    inner = 2.0 * double - exact(exact(double, correlation, ROW_BY_COL), double, ROW_BY_COL)

    for step in range(1, cols):
        source = (col + cols - step) % cols
        arrive(stat_cols.at[source], scol_recv.at[source])
    total = stat_cols[0]
    for source in range(1, cols):
        total += stat_cols[source]
    stat_rows[row] = total
    last_sent = []
    for step in FAR_FIRST:
        peer = row_after(row, step)
        last_sent.append(to_row(stat_rows.at[row], stat_rows.at[row], srow_send.at[step], srow_recv.at[row], peer))
    for copy in sent:
        copy.wait_send()
    sent = []

    @pl.loop(1, rows)
    def _(step):
        arrive(image_out.at[row_after(row, far_first(step))], image_send.at[step])

    for step in range(1, rows):
        source = row_before(row, step)
        arrive(squares.at[source], square_recv.at[source])
    square = squares[0]
    for source in range(1, rows):
        square += squares[source]

    for step in FAR_FIRST:
        source = row_before(row, step)
        arrive(stat_rows.at[source], srow_recv.at[source])
    total = stat_rows[0]
    for source in range(1, rows):
        total += stat_rows[source]
    cross = jnp.concatenate([total[:, : prior - BS], square[:, :BS]], 1)
    self_gram = total[:, prior - BS :]
    coeffs = exact(cross, double, ROW_BY_ROW)
    gram = self_gram - exact(exact(cross, inner, ROW_BY_ROW), cross, ROW_BY_ROW)
    image -= exact(coeffs, own, ROW_BY_COL)
    coef_ref[...] = coeffs

    line = lax.broadcasted_iota(jnp.int32, (BS, BS), 0)
    lane = lax.broadcasted_iota(jnp.int32, (BS, BS), 1)
    below = lax.broadcasted_iota(jnp.int32, (BS, 1), 0)
    factor = jnp.zeros((BS, BS), f32)
    for j in range(BS):
        column = gram[:, j : j + 1]
        scale = lax.rsqrt(column[j : j + 1])
        column = column * scale
        gram_line = gram[j : j + 1] * scale
        image_line = image[j : j + 1] * scale
        factor = jnp.where((lane == j) & (line >= j), column, factor)
        part = jnp.where(below > j, column, 0.0)
        gram = gram - part * gram_line
        image = jnp.where(below == j, image_line, image - part * image_line)
    new_ref[...] = image
    factor_ref[...] = factor

    for copy in last_sent:
        copy.wait_send()


def local(rows, cols, projection, basis):
    rays, columns = projection.shape
    prior, width = basis.shape
    dma = pltpu.SemaphoreType.DMA
    call = pl.pallas_call(
        functools.partial(kernel, rows, cols),
        out_shape=(
            jax.ShapeDtypeStruct((BS, width), f32),
            jax.ShapeDtypeStruct((BS, prior), f32),
            jax.ShapeDtypeStruct((BS, BS), f32),
        ),
        in_specs=[pl.BlockSpec(memory_space=pltpu.HBM)] * 2,
        out_specs=[pl.BlockSpec(memory_space=pltpu.VMEM)] * 3,
        scratch_shapes=[
            pltpu.VMEM((DEPTH, rays, width), f32),
            pltpu.VMEM((rows, rays, width), bf16),
            pltpu.VMEM((rows, rays, width), bf16),
            pltpu.VMEM((rows, width, rays), bf16),
            pltpu.VMEM((rows, width, rays), bf16),
            pltpu.VMEM((prior, width), f32),
            pltpu.VMEM((rows, BS, width), f32),
            pltpu.VMEM((BS, rays), f32),
            pltpu.VMEM((2, cols, BS, rays // 2), f32),
            pltpu.VMEM((rows, BS, width), f32),
            pltpu.VMEM((rows, BS, width), f32),
            pltpu.VMEM((cols, prior // cols, prior), f32),
            pltpu.VMEM((cols, prior // cols, prior), f32),
            pltpu.VMEM((rows, prior // cols, prior), f32),
            pltpu.VMEM((cols, prior // cols, prior), f32),
            pltpu.VMEM((cols, BS, prior), f32),
            pltpu.VMEM((rows, BS, prior), f32),
            pltpu.VMEM((rows, BS, prior), f32),
            dma((DEPTH,)), dma,
            dma((rows,)), dma((rows,)),
            dma((2, cols)), dma((2, cols)),
            dma((rows,)), dma((rows,)),
            dma((cols,)), dma((cols,)), dma((rows,)), dma((rows,)), dma((cols,)), dma((cols,)),
            dma((cols,)), dma((cols,)), dma((rows,)), dma((rows,)), dma((rows,)), dma((rows,)),
        ],
        compiler_params=pltpu.CompilerParams(
            collective_id=0, has_side_effects=True, vmem_limit_bytes=55040 << 10
        ),
    )
    new_block, coefficients, factor = call(projection, basis)
    return new_block, coefficients.T, factor


def solution(mesh):
    placed = (P("rows", "cols"), P(None, ("cols", "rows")))
    return jax.shard_map(
        functools.partial(local, mesh.shape["rows"], mesh.shape["cols"]),
        mesh=mesh,
        in_specs=placed,
        out_specs=(P(None, ("cols", "rows")), P(), P()),
        check_vma=False,
    )
```
